128 devices in a mesh: gx: 8 (over z, x_lo), gy: 16 (over y, x_hi, core).
Axes of the slice: x: 4 (x_hi: 2, x_lo: 2; x = x_hi * 2 + x_lo), y: 4, z: 4, core: 2. Of those that a mesh axis runs over, the one named last changes fastest.
Arguments:
- increments: float32 [2, 3, 384, 2048], P(None, None, 'gy', 'gx'), may hold values from -6 to 6
- diffusivity: float32 [3, 384, 2048], P(None, 'gy', 'gx'), may hold values from 0.02 to 0.24
- sea_mask: int32 [384, 2048], P('gy', 'gx'), may hold values 0 or 1
- source_cells: int32 [128, 128, 3, 8, 128], P(('gx', 'gy')), may hold values from 0 to 255, as said below
- source_weights: float32 [128, 128, 8, 128], P(('gx', 'gy')), may hold values from 0.1 to 1
- source_counts: int32 [128, 128, 128], P(('gx', 'gy')), may hold values from 0 to 8
- slot_owner: int32 [128, 128, 128], P(('gx', 'gy')), may hold values from 0 to 4095
Outputs:
- smoothed: float32 [2, 3, 384, 2048], P(None, None, 'gy', 'gx')
- obs_equiv: float32 [524288], P(('gx', 'gy'))
The draws below stay inside these ranges and needn't reach their ends.
Inputs may be any that keep to these rules, and one draw needn't show every extreme that they name: `source_cells`: component 0 is a layer below 6, component 1 a row below 24, component 2 a column below 256, all within the grid device's own tile. `source_counts`: number of leading valid entries of the slot; 0 leaves the slot empty. `slot_owner`: an observation index local to the owner.
All inputs are finite; a program needn't handle non-finite values. No bound on the sum of `sea_mask` on one device may be relied on, other than what follows from the above.
Results may differ from the reference program's by a relative error of at most 0.00002.
Values sent between devices are 32-bit elements; how exact they have to be, the bound alone decides.
No kernel may reach another device: no remote copies, remote signals or barrier semaphores. Data moves between devices by JAX's collectives and lax.ppermute only.
A program may use at most 64 MiB of HBM per device.

```python
import math
import jax
import jax.numpy as jnp
from jax import lax

FIELDS = 2
LEVELS = 3
ITERS = 10
CY = 24
CX = 256
OBS_DEV = 4096
SLOTS = 128
NY = 384
NX = 2048
NOBS = 524288
N_GY = 16
DEVICES = 128


def draw_source_cells(key, part):
    key_layer, key_row, key_col = jax.random.split(key, 3)
    shape = (DEVICES, DEVICES, 1, 8, SLOTS)
    layer = jax.random.randint(key_layer, shape, 0, FIELDS * LEVELS, dtype=jnp.int32)
    row_pick = jax.random.randint(key_row, shape, 0, CY, dtype=jnp.int32)
    col_pick = jax.random.randint(key_col, shape, 0, CX, dtype=jnp.int32)
    return jnp.concatenate([layer, row_pick, col_pick], axis=2)


def with_ends(entries, rng, low, largest):
    extent = entries.shape
    spot = [jax.random.randint(jax.random.fold_in(rng, axis), (), 0, extent[axis]) for axis in range(len(extent))]
    entries = entries.at[tuple(spot)].set(low)
    longest = extent.index(max(extent))
    spot[longest] = (spot[longest] + 1) % extent[longest]
    return entries.at[tuple(spot)].set(largest)


def block_scale(own_key, dims, cuts, least, top_value):
    level = 1.0
    for dim, parts in cuts:
        steps = jax.random.uniform(jax.random.fold_in(jax.random.fold_in(own_key, 6), dim), (parts,), jnp.float32, least / len(cuts), top_value / len(cuts))
        level = level * jnp.repeat(jnp.exp(steps), dims[dim] // parts).reshape((-1,) + (1,) * (len(dims) - 1 - dim))
    return level


def centred(own_key, dims, deviation, limit, cuts=(), held_as=jnp.bfloat16):
    values = deviation * jax.random.normal(own_key, dims, jnp.float32)
    if cuts:
        values = values * block_scale(own_key, dims, cuts, -0.22, 0.18)
    return jnp.clip(values, -limit, limit).astype(held_as)


def setup_inputs(seed: int = 0) -> dict:
    arg_keys = jax.random.split(jax.random.key(seed), 8)
    increments = centred(arg_keys[0], (FIELDS, LEVELS, NY, NX), 1.0, 6.0, ((2, 16), (3, 8)), jnp.float32)
    diffusivity = jnp.clip(jnp.exp(math.log(0.24) - 2.4849066 * jax.random.uniform(arg_keys[1], (LEVELS, NY, NX), jnp.float32) ** block_scale(arg_keys[1], (LEVELS, NY, NX), ((1, 16), (2, 8)), -0.2, 0.2)), 0.02, 0.24)
    sea_mask = with_ends((jax.random.randint(arg_keys[2], (NY, NX), 0, 10) < 7).astype(jnp.int32), jax.random.fold_in(arg_keys[2], 1), 0, 1)
    source_cells = draw_source_cells(jax.random.fold_in(arg_keys[7], 71), 0)
    source_weights = jnp.clip(0.1 + 0.9 * jax.random.uniform(arg_keys[4], (DEVICES, DEVICES, 8, SLOTS), jnp.float32) ** block_scale(arg_keys[4], (DEVICES, DEVICES, 8, SLOTS), ((0, 128),), -0.2, 0.2), 0.1, 1.0)
    source_counts = with_ends(jax.random.randint(arg_keys[5], (DEVICES, DEVICES, SLOTS), 0, 9), jax.random.fold_in(arg_keys[5], 1), 0, 8).astype(jnp.int32)
    slot_owner = with_ends(jax.random.randint(arg_keys[6], (DEVICES, DEVICES, SLOTS), 0, OBS_DEV), jax.random.fold_in(arg_keys[6], 1), 0, OBS_DEV - 1).astype(jnp.int32)
    return dict(increments=increments, diffusivity=diffusivity, sea_mask=sea_mask, source_cells=source_cells, source_weights=source_weights, source_counts=source_counts, slot_owner=slot_owner)


def shift_east(array):
    return jnp.roll(array, -1, axis=-1)


def shift_west(array):
    return jnp.roll(array, 1, axis=-1)


def shift_north(array):
    return jnp.concatenate([array[..., 1:, :], jnp.zeros_like(array[..., :1, :])], axis=-2)


def shift_south(array):
    return jnp.concatenate([jnp.zeros_like(array[..., :1, :]), array[..., :-1, :]], axis=-2)


def reference(increments, diffusivity, sea_mask, source_cells, source_weights, source_counts, slot_owner):
    wet = sea_mask.astype(jnp.float32)

    def smooth_level(pair):
        level_fields, diffuse = pair
        c_east = 0.5 * (diffuse + shift_east(diffuse)) * wet * shift_east(wet)
        c_west = 0.5 * (diffuse + shift_west(diffuse)) * wet * shift_west(wet)
        c_north = 0.5 * (diffuse + shift_north(diffuse)) * wet * shift_north(wet)
        c_south = 0.5 * (diffuse + shift_south(diffuse)) * wet * shift_south(wet)
        field = level_fields * wet
        for turn_index in range(ITERS):
            field = field + (c_east * (shift_east(field) - field) - c_west * (field - shift_west(field))) + (c_north * (shift_north(field) - field) - c_south * (field - shift_south(field)))
        return field

    by_level = lax.map(smooth_level, (jnp.transpose(increments, (1, 0, 2, 3)), diffusivity))
    smoothed = jnp.transpose(by_level, (1, 0, 2, 3))
    device_ids = jnp.arange(DEVICES, dtype=jnp.int32)[:, None, None, None]
    lon_block = device_ids // N_GY
    lat_block = device_ids % N_GY
    layer = source_cells[:, :, 0]
    row_index = source_cells[:, :, 1]
    col_index = source_cells[:, :, 2]
    global_flat = layer * (NY * NX) + (lat_block * CY + row_index) * NX + lon_block * CX + col_index
    values = smoothed.reshape(-1)[global_flat.astype(jnp.int32)]
    valid = jnp.arange(8, dtype=jnp.int32)[None, None, :, None] < source_counts[:, :, None, :]
    partial_value = jnp.sum(jnp.where(valid, source_weights * values, jnp.float32(0.0)), axis=2)
    owner_ids = jnp.arange(DEVICES, dtype=jnp.int32)[:, None, None]
    targets = owner_ids * OBS_DEV + slot_owner
    obs_equiv = jnp.zeros((NOBS,), jnp.float32).at[targets.reshape(-1)].add(jnp.transpose(partial_value, (1, 0, 2)).reshape(-1))
    return smoothed, obs_equiv
```

```python
import jax
import jax.numpy as jnp
from jax import lax
from jax.experimental import pallas as pl
from jax.experimental.pallas import tpu as pltpu
from jax.sharding import PartitionSpec as P

F32 = jnp.float32
BF16 = jnp.bfloat16
ITERS = 10
HALO = 10
OBS_DEV = 4096
LAYERS = 6
LEVELS = 3
ARRAYS = LAYERS + LEVELS
CY = 24
CX = 256
LANES = 128
STRIDE = 14
ROWS = 48
COLS = 384
TABLE = LAYERS * CY * 2
TURN = 8
OWNERS = 128
BLOCK = 32


def iota(shape, dim):
    return lax.broadcasted_iota(jnp.int32, shape, dim)


def pack_kernel(inc_ref, dif_ref, mask_ref, base_ref, first_ref, last_ref):
    wet = mask_ref[...].astype(F32)
    lane = iota((CY, LANES), 1)
    first = jnp.zeros((CY, LANES), F32)
    last = jnp.zeros((CY, LANES), F32)
    for a in range(ARRAYS):
        values = (inc_ref[a] if a < LAYERS else dif_ref[a - LAYERS]) * wet
        base_ref[a] = values
        mine = (lane >= STRIDE * a) & (lane < STRIDE * a + HALO)
        left = values[:, :LANES]
        right = values[:, LANES:]
        if a:
            left = pltpu.roll(left, STRIDE * a, 1)
        right = pltpu.roll(right, STRIDE * a + HALO, 1)
        first = jnp.where(mine, left, first)
        last = jnp.where(mine, right, last)
    first_ref[...] = first
    last_ref[...] = last


def rows_kernel(base_ref, east_ref, west_ref, low_ref, high_ref):
    for a in range(ARRAYS + 1):
        for ref, start in ((low_ref, 0), (high_ref, CY - HALO)):
            if a < ARRAYS:
                ref[pl.ds(HALO * a, HALO), :] = base_ref[a, pl.ds(start, HALO), :]
            else:
                ref[pl.ds(HALO * a, HALO), pl.ds(0, LANES)] = east_ref[pl.ds(start, HALO), :]
                ref[pl.ds(HALO * a, HALO), pl.ds(LANES, LANES)] = west_ref[pl.ds(start, HALO), :]


def smooth(base_ref, east_ref, west_ref, north_ref, south_ref, wide_ref, across_ref, up_ref, out_ref):
    lane_tile = iota((CY, LANES), 1)
    lane_rows = iota((HALO, LANES), 1)

    def side(east, west, a, lane):
        if a:
            east = pltpu.roll(east, LANES - STRIDE * a, 1)
        west = pltpu.roll(west, (LANES - HALO - STRIDE * a) % LANES, 1)
        halo = jnp.where(lane < HALO, east, 0.0)
        return jnp.where(lane >= LANES - HALO, west, halo)

    strip = pl.ds(HALO * ARRAYS, HALO)
    for a in range(ARRAYS):
        wide_ref[a, pl.ds(0, CY), pl.ds(0, CX)] = base_ref[a]
        wide_ref[a, pl.ds(0, CY), pl.ds(CX, LANES)] = side(east_ref[...], west_ref[...], a, lane_tile)
        wide_ref[a, pl.ds(CY, CY), :] = jnp.zeros((CY, COLS), F32)
        for ref, start in ((north_ref, CY), (south_ref, ROWS - HALO)):
            wide_ref[a, pl.ds(start, HALO), pl.ds(0, CX)] = ref[pl.ds(HALO * a, HALO), :]
            wide_ref[a, pl.ds(start, HALO), pl.ds(CX, LANES)] = side(
                ref[strip, pl.ds(0, LANES)], ref[strip, pl.ds(LANES, LANES)], a, lane_rows
            )
    for level in range(LEVELS):
        here = wide_ref[LAYERS + level]
        for ref, axis, size in ((across_ref, 1, COLS), (up_ref, 0, ROWS)):
            there = pltpu.roll(here, size - 1, axis)
            both = (here > 0.0) & (there > 0.0)
            ref[level] = jnp.where(both, 0.5 * (here + there), 0.0)

    def one_layer(layer, _):
        level = layer % LEVELS

        def turn(_, field):
            east = across_ref[level] * (pltpu.roll(field, COLS - 1, 1) - field)
            north = up_ref[level] * (pltpu.roll(field, ROWS - 1, 0) - field)
            return field + (east - pltpu.roll(east, 1, 1)) + (north - pltpu.roll(north, 1, 0))

        field = lax.fori_loop(0, ITERS, turn, wide_ref[layer])
        out_ref[layer] = field[:CY, :CX]
        return 0

    lax.fori_loop(0, LAYERS, one_layer, 0)


def choose(parts, bits):
    turn = 0
    while len(parts) > 1:
        pairs = [
            jnp.where(bits[turn], parts[2 * j + 1], parts[2 * j]) for j in range(len(parts) // 2)
        ]
        parts = pairs + parts[2 * len(pairs):]
        turn += 1
    return parts[0]


def main_kernel(
    base_ref, east_ref, west_ref, north_ref, south_ref, cells_ref, weights_ref, counts_ref,
    smooth_ref, partial_ref, wide_ref, across_ref, up_ref, table_ref,
):
    @pl.when(pl.program_id(0) == 0)
    def _():
        smooth(
            base_ref, east_ref, west_ref, north_ref, south_ref, wide_ref, across_ref, up_ref,
            smooth_ref,
        )
        for half in range(2):
            for layer in range(LAYERS):
                values = smooth_ref[layer, :, pl.ds(half * LANES, LANES)]
                coarse = values.astype(BF16)
                fine = (values - coarse.astype(F32)).astype(BF16)
                rows = pl.ds((half * LAYERS + layer) * CY, CY)
                table_ref[rows, pl.ds(0, LANES)] = coarse.astype(F32)
                table_ref[rows, pl.ds(LANES, LANES)] = fine.astype(F32)

    table = table_ref[...].astype(BF16)
    lane_id = iota((LANES, LANES), 0).astype(BF16)
    sub_id = iota((8, LANES), 0)

    def one_owner(o):
        layer = cells_ref[o, 0]
        row = cells_ref[o, 1]
        col = cells_ref[o, 2]
        rows_at = (col >> 7) * (LAYERS * CY) + layer * CY + row
        lane_at = (col & (LANES - 1)).astype(F32).astype(BF16)
        weights = jnp.where(sub_id < counts_ref[pl.ds(o, 1), :], weights_ref[o], 0.0)
        total = jnp.zeros((8, LANES), F32)
        for k in range(0, 8, 2):
            picks = []
            for j in (k, k + 1):
                lane_row = jnp.broadcast_to(lane_at[j:j + 1, :], (LANES, LANES))
                picks.append(jnp.where(lane_id == lane_row, BF16(1), BF16(0)))
            pick = jnp.concatenate(picks, axis=1)
            found = jnp.dot(
                table, jnp.concatenate([pick, pick], axis=0), preferred_element_type=F32
            )
            for j in (0, 1):
                block = found[:, j * LANES:(j + 1) * LANES]
                at = jnp.broadcast_to(rows_at[k + j:k + j + 1, :], (8, LANES))
                bits = [(at & (8 << b)) != 0 for b in range(6)]
                value = choose([block[8 * q:8 * q + 8] for q in range(TABLE // 8)], bits)
                value = jnp.where(sub_id == (at & 7), value, 0.0)
                total = total + value * jnp.broadcast_to(weights[k + j:k + j + 1, :], (8, LANES))
        partial_ref[o] = jnp.sum(total, axis=0, keepdims=True)

    def some(i, _):
        for j in range(TURN):
            one_owner(i * TURN + j)
        return 0

    lax.fori_loop(0, BLOCK // TURN, some, 0)


def owner_kernel(values_ref, slots_ref, out_ref):
    high_id = iota((32, LANES), 0)
    low_id = iota((LANES, LANES), 0)
    total = jnp.zeros((64, LANES), F32)
    for g in range(0, OWNERS, 8):
        left = []
        right = []
        for j in range(g, g + 8):
            value = values_ref[j]
            slot = slots_ref[pl.ds(j, 1), :]
            coarse = value.astype(BF16).astype(F32)
            fine = value - coarse
            high = high_id == (slot >> 7)
            left.append(
                jnp.concatenate([jnp.where(high, coarse, 0.0), jnp.where(high, fine, 0.0)], axis=0)
            )
            right.append(jnp.where(low_id == (slot & 127), 1.0, 0.0))
        total = total + lax.dot_general(
            jnp.concatenate(left, axis=1).astype(BF16),
            jnp.concatenate(right, axis=1).astype(BF16),
            (((1,), (1,)), ((), ())),
            preferred_element_type=F32,
        )
    out_ref[...] = total[:32] + total[32:]


def shape(*dims):
    return jax.ShapeDtypeStruct(dims, F32)


def shift(array, axis, step, wrap):
    size = lax.axis_size(axis)
    pairs = [(i, (i + step) % size) for i in range(size) if wrap or 0 <= i + step < size]
    return lax.ppermute(array, axis, pairs)


def whole(*dims):
    return pl.BlockSpec(dims, lambda i: (0,) * len(dims))


def local(
    increments, diffusivity, sea_mask, source_cells, source_weights, source_counts, slot_owner
):
    base, first, last = pl.pallas_call(
        pack_kernel,
        out_shape=(shape(ARRAYS, CY, CX), shape(CY, LANES), shape(CY, LANES)),
        name="pack",
    )(increments.reshape(LAYERS, CY, CX), diffusivity, sea_mask)
    east = shift(first, "gx", -1, True)
    west = shift(last, "gx", 1, True)
    low, high = pl.pallas_call(
        rows_kernel,
        out_shape=(shape(HALO * (ARRAYS + 1), CX), shape(HALO * (ARRAYS + 1), CX)),
        name="rows",
    )(base, east, west)
    north = shift(low, "gy", -1, False)
    south = shift(high, "gy", 1, False)
    strip = (HALO * (ARRAYS + 1), CX)
    smoothed, partial_value = pl.pallas_call(
        main_kernel,
        grid=(OWNERS // BLOCK,),
        in_specs=[
            whole(ARRAYS, CY, CX),
            whole(CY, LANES),
            whole(CY, LANES),
            whole(*strip),
            whole(*strip),
            pl.BlockSpec((BLOCK, 3, 8, LANES), lambda i: (i, 0, 0, 0)),
            pl.BlockSpec((BLOCK, 8, LANES), lambda i: (i, 0, 0)),
            pl.BlockSpec((BLOCK, LANES), lambda i: (i, 0)),
        ],
        out_specs=(whole(LAYERS, CY, CX), pl.BlockSpec((BLOCK, 1, LANES), lambda i: (i, 0, 0))),
        out_shape=(shape(LAYERS, CY, CX), shape(OWNERS, 1, LANES)),
        scratch_shapes=[
            pltpu.VMEM((ARRAYS, ROWS, COLS), F32),
            pltpu.VMEM((LEVELS, ROWS, COLS), F32),
            pltpu.VMEM((LEVELS, ROWS, COLS), F32),
            pltpu.VMEM((TABLE, 2 * LANES), F32),
        ],
        name="main",
    )(base, east, west, north, south, source_cells[0], source_weights[0], source_counts[0])
    received = lax.all_to_all(
        partial_value, ("gx", "gy"), split_axis=0, concat_axis=0, tiled=True
    )
    obs_equiv = pl.pallas_call(
        owner_kernel, out_shape=shape(OBS_DEV // LANES, LANES), name="owner"
    )(received, slot_owner[0])
    return smoothed.reshape(increments.shape), obs_equiv.reshape(-1)


def solution(mesh):
    return jax.shard_map(
        local,
        mesh=mesh,
        in_specs=(
            P(None, None, "gy", "gx"),
            P(None, "gy", "gx"),
            P("gy", "gx"),
            P(("gx", "gy"), None, None, None, None),
            P(("gx", "gy"), None, None, None),
            P(("gx", "gy"), None, None),
            P(("gx", "gy"), None, None),
        ),
        out_specs=(P(None, None, "gy", "gx"), P(("gx", "gy"))),
        check_vma=False,
    )
```

```python
import jax
import jax.numpy as jnp
from jax import lax
from jax.experimental import pallas as pl
from jax.experimental.pallas import tpu as pltpu
from jax.sharding import PartitionSpec as P

F32 = jnp.float32
BF16 = jnp.bfloat16
ITERS = 10
HALO = 10
OBS_DEV = 4096
LAYERS = 6
LEVELS = 3
ARRAYS = LAYERS + LEVELS
CY = 24
CX = 256
LANES = 128
STRIDE = 14
ROWS = 48
WIDE = 3
TABLE = LAYERS * CY * 2
TURN = 16
LOOKED_UP = 4
BANDS = 6
UNROLL = 5
OWNERS = 128
VMEM = pl.BlockSpec(memory_space=pltpu.VMEM)


def iota(shape, dim):
    return lax.broadcasted_iota(jnp.int32, shape, dim)


def pack_kernel(inc_ref, dif_ref, mask_ref, base_ref, first_ref, last_ref):
    wet = mask_ref[...].astype(F32)
    lane = iota((CY, LANES), 1)
    first = jnp.zeros((CY, LANES), F32)
    last = jnp.zeros((CY, LANES), F32)
    for a in range(ARRAYS):
        values = (inc_ref[a] if a < LAYERS else dif_ref[a - LAYERS]) * wet
        base_ref[a] = values
        mine = (lane >= STRIDE * a) & (lane < STRIDE * a + HALO)
        left = values[:, :LANES]
        right = values[:, LANES:]
        if a:
            left = pltpu.roll(left, STRIDE * a, 1)
        right = pltpu.roll(right, STRIDE * a + HALO, 1)
        first = jnp.where(mine, left, first)
        last = jnp.where(mine, right, last)
    first_ref[...] = first
    last_ref[...] = last


def rows_kernel(base_ref, east_ref, west_ref, low_ref, high_ref):
    for a in range(ARRAYS + 1):
        for ref, start in ((low_ref, 0), (high_ref, CY - HALO)):
            if a < ARRAYS:
                ref[pl.ds(HALO * a, HALO), :] = base_ref[a, pl.ds(start, HALO), :]
            else:
                ref[pl.ds(HALO * a, HALO), pl.ds(0, LANES)] = east_ref[pl.ds(start, HALO), :]
                ref[pl.ds(HALO * a, HALO), pl.ds(LANES, LANES)] = west_ref[pl.ds(start, HALO), :]


def smooth(
    base_ref, east_ref, west_ref, north_ref, south_ref, out_ref, wide_ref, coeff_ref,
    table_ref,
):
    lane_tile = iota((CY, LANES), 1)
    lane_rows = iota((HALO, LANES), 1)

    def side(east, west, a, lane):
        if a:
            east = pltpu.roll(east, LANES - STRIDE * a, 1)
        west = pltpu.roll(west, (LANES - HALO - STRIDE * a) % LANES, 1)
        halo = jnp.where(lane < HALO, east, 0.0)
        return jnp.where(lane >= LANES - HALO, west, halo)

    strip = pl.ds(HALO * ARRAYS, HALO)
    for a in range(ARRAYS):
        for v in range(2):
            lanes = pl.ds(v * LANES, LANES)
            wide_ref[a, v, pl.ds(0, CY), :] = base_ref[a, :, lanes]
            wide_ref[a, v, pl.ds(CY, CY), :] = jnp.zeros((CY, LANES), F32)
            wide_ref[a, v, pl.ds(CY, HALO), :] = north_ref[pl.ds(HALO * a, HALO), lanes]
            wide_ref[a, v, pl.ds(ROWS - HALO, HALO), :] = south_ref[pl.ds(HALO * a, HALO), lanes]
        wide_ref[a, 2, pl.ds(0, CY), :] = side(east_ref[...], west_ref[...], a, lane_tile)
        wide_ref[a, 2, pl.ds(CY, CY), :] = jnp.zeros((CY, LANES), F32)
        for ref, start in ((north_ref, CY), (south_ref, ROWS - HALO)):
            wide_ref[a, 2, pl.ds(start, HALO), :] = side(
                ref[strip, pl.ds(0, LANES)], ref[strip, pl.ds(LANES, LANES)], a, lane_rows
            )

    lane = iota((8, LANES), 1)

    def bands(a):
        return [
            [wide_ref[a, v, pl.ds(b, 8, stride=BANDS), :] for v in range(WIDE)]
            for b in range(BANDS)
        ]

    def to_east(parts):
        turned = [pltpu.roll(part, LANES - 1, 1) for part in parts]
        return [
            jnp.where(lane == LANES - 1, turned[(v + 1) % WIDE], turned[v]) for v in range(WIDE)
        ]

    def to_west(parts):
        turned = [pltpu.roll(part, 1, 1) for part in parts]
        return [jnp.where(lane == 0, turned[(v - 1) % WIDE], turned[v]) for v in range(WIDE)]

    def to_north(values):
        return values[1:] + [[pltpu.roll(part, 7, 0) for part in values[0]]]

    def to_south(values):
        return [[pltpu.roll(part, 1, 0) for part in values[-1]]] + values[:-1]

    def face(here, there):
        return [
            jnp.where((x > 0.0) & (y > 0.0), 0.5 * (x + y), 0.0) for x, y in zip(here, there)
        ]

    for level in range(LEVELS):
        here = bands(LAYERS + level)
        north = [face(x, y) for x, y in zip(here, to_north(here))]
        south = to_south(north)
        for b in range(BANDS):
            east = face(here[b], to_east(here[b]))
            west = to_west(east)
            for v in range(WIDE):
                sides = (east[v], west[v], north[b][v], south[b][v])
                keep = 1.0 - ((sides[0] + sides[1]) + (sides[2] + sides[3]))
                for i, side_value in enumerate((keep,) + sides):
                    coeff_ref[level, i, b, v] = side_value

    def step(field, level):
        north = to_north(field)
        south = to_south(field)
        updated = []
        for b in range(BANDS):
            around = (field[b], to_east(field[b]), to_west(field[b]), north[b], south[b])
            parts = []
            for v in range(WIDE):
                terms = [coeff_ref[level, i, b, v] * near[v] for i, near in enumerate(around)]
                parts.append(terms[0] + ((terms[1] + terms[2]) + (terms[3] + terms[4])))
            updated.append(parts)
        return updated

    for level in range(LEVELS):

        def turn(_, fields):
            for _ in range(UNROLL):
                fields = [step(field, level) for field in fields]
            return fields

        pair = lax.fori_loop(0, ITERS // UNROLL, turn, [bands(level), bands(level + LEVELS)])
        for layer, field in zip((level, level + LEVELS), pair):
            for v in range(2):
                first = (v * LAYERS + layer) * CY
                for b in range(BANDS):
                    table_ref[pl.ds(first + b, CY // BANDS, stride=BANDS), :] = field[b][v][
                        :CY // BANDS
                    ]
                out_ref[layer, :, pl.ds(v * LANES, LANES)] = table_ref[pl.ds(first, CY), :]


def choose(parts, bits):
    turn = 0
    while len(parts) > 1:
        pairs = [
            jnp.where(bits[turn], parts[2 * j + 1], parts[2 * j]) for j in range(len(parts) // 2)
        ]
        parts = pairs + parts[2 * len(pairs):]
        turn += 1
    return parts[0]


def main_kernel(
    base_ref, east_ref, west_ref, north_ref, south_ref, cells_far, weights_far, counts_far,
    smooth_ref, partial_ref, wide_ref, coeff_ref, table_ref, split_ref, cells_ref, weights_ref,
    counts_ref, arrived,
):
    fetches = [
        pltpu.make_async_copy(far, ref, arrived.at[i])
        for i, (far, ref) in enumerate(
            ((cells_far, cells_ref), (weights_far, weights_ref), (counts_far, counts_ref))
        )
    ]
    for fetch in fetches:
        fetch.start()
    smooth(
        base_ref, east_ref, west_ref, north_ref, south_ref, smooth_ref, wide_ref, coeff_ref,
        table_ref,
    )
    values = table_ref[...]
    coarse = values.astype(BF16)
    split_ref[:, pl.ds(0, LANES)] = coarse
    split_ref[:, pl.ds(LANES, LANES)] = (values - coarse.astype(F32)).astype(BF16)

    for fetch in fetches:
        fetch.wait()
    split = split_ref[...]
    lane_id = iota((LANES, LANES), 0).astype(BF16)
    sub_id = iota((8, LANES), 0)

    def places(o):
        col = cells_ref[o, 2]
        rows_at = (col >> 7) * (LAYERS * CY) + cells_ref[o, 0] * CY + cells_ref[o, 1]
        weights = jnp.where(sub_id < counts_ref[pl.ds(o, 1), :], weights_ref[o], 0.0)
        return rows_at, col & (LANES - 1), weights

    def by_matmul(o):
        rows_at, lane_at, weights = places(o)
        lane_at = lane_at.astype(F32).astype(BF16)
        total = jnp.zeros((8, LANES), F32)
        for k in range(0, 8, 2):
            picks = []
            for j in (k, k + 1):
                lane_row = jnp.broadcast_to(lane_at[j:j + 1, :], (LANES, LANES))
                picks.append(jnp.where(lane_id == lane_row, BF16(1), BF16(0)))
            pick = jnp.concatenate(picks, axis=1)
            found = jnp.dot(
                split, jnp.concatenate([pick, pick], axis=0), preferred_element_type=F32
            )
            for j in (0, 1):
                block = found[:, j * LANES:(j + 1) * LANES]
                at = jnp.broadcast_to(rows_at[k + j:k + j + 1, :], (8, LANES))
                bits = [(at & (8 << b)) != 0 for b in range(6)]
                value = choose([block[8 * q:8 * q + 8] for q in range(TABLE // 8)], bits)
                value = jnp.where(sub_id == (at & 7), value, 0.0)
                total = total + value * jnp.broadcast_to(weights[k + j:k + j + 1, :], (8, LANES))
        partial_ref[o] = jnp.sum(total, axis=0, keepdims=True)

    def by_lanes(owners):
        spots = [places(o) for o in owners]
        bits = [[(rows_at & (1 << b)) != 0 for b in range(3)] for rows_at, _, _ in spots]
        found = [jnp.zeros((8, LANES), F32) for _ in owners]
        for q in range(TABLE // 8):
            rows = [table_ref[pl.ds(8 * q + r, 8, stride=0), :] for r in range(8)]
            for i, (rows_at, lane_at, _) in enumerate(spots):
                value = choose([jnp.take_along_axis(row, lane_at, axis=1) for row in rows], bits[i])
                found[i] = jnp.where((rows_at >> 3) == q, value, found[i])
        for o, value, (_, _, weights) in zip(owners, found, spots):
            partial_ref[o] = jnp.sum(value * weights, axis=0, keepdims=True)

    def some(i, _):
        first = i * TURN
        for j in range(TURN - LOOKED_UP):
            by_matmul(first + j)
        for j in range(TURN - LOOKED_UP, TURN, 2):
            by_lanes((first + j, first + j + 1))
        return 0

    lax.fori_loop(0, OWNERS // TURN, some, 0)


def owner_kernel(values_ref, slots_ref, out_ref):
    high_id = iota((32, LANES), 0)
    low_id = iota((LANES, LANES), 0)
    total = jnp.zeros((64, LANES), F32)
    for g in range(0, OWNERS, 8):
        left = []
        right = []
        for j in range(g, g + 8):
            value = values_ref[j]
            slot = slots_ref[pl.ds(j, 1), :]
            coarse = value.astype(BF16).astype(F32)
            fine = value - coarse
            high = high_id == (slot >> 7)
            left.append(
                jnp.concatenate([jnp.where(high, coarse, 0.0), jnp.where(high, fine, 0.0)], axis=0)
            )
            right.append(jnp.where(low_id == (slot & 127), 1.0, 0.0))
        total = total + lax.dot_general(
            jnp.concatenate(left, axis=1).astype(BF16),
            jnp.concatenate(right, axis=1).astype(BF16),
            (((1,), (1,)), ((), ())),
            preferred_element_type=F32,
        )
    out_ref[...] = total[:32] + total[32:]


def shape(*dims):
    return jax.ShapeDtypeStruct(dims, F32)


def shift(array, axis, step, wrap):
    size = lax.axis_size(axis)
    pairs = [(i, (i + step) % size) for i in range(size) if wrap or 0 <= i + step < size]
    return lax.ppermute(array, axis, pairs)


def near(*arrays):
    return [pltpu.with_memory_space_constraint(array, pltpu.MemorySpace.VMEM) for array in arrays]


def local(
    increments, diffusivity, sea_mask, source_cells, source_weights, source_counts, slot_owner
):
    base, first, last = pl.pallas_call(
        pack_kernel,
        in_specs=[VMEM] * 3,
        out_specs=(VMEM,) * 3,
        out_shape=(pltpu.VMEM((ARRAYS, CY, CX), F32),) + (pltpu.VMEM((CY, LANES), F32),) * 2,
        name="pack",
    )(increments.reshape(LAYERS, CY, CX), diffusivity, sea_mask)
    east = shift(first, "gx", -1, True)
    west = shift(last, "gx", 1, True)
    low, high = pl.pallas_call(
        rows_kernel,
        in_specs=[VMEM] * 3,
        out_specs=(VMEM,) * 2,
        out_shape=(pltpu.VMEM((HALO * (ARRAYS + 1), CX), F32),) * 2,
        name="rows",
    )(*near(base, east, west))
    north = shift(low, "gy", -1, False)
    south = shift(high, "gy", 1, False)
    smoothed, partial_value = pl.pallas_call(
        main_kernel,
        in_specs=[VMEM] * 5 + [pl.BlockSpec(memory_space=pl.ANY)] * 3,
        out_specs=(VMEM,) * 2,
        out_shape=(shape(LAYERS, CY, CX), pltpu.VMEM((OWNERS, 1, LANES), F32)),
        scratch_shapes=[
            pltpu.VMEM((ARRAYS, WIDE, ROWS, LANES), F32),
            pltpu.VMEM((LEVELS, 5, BANDS, WIDE, 8, LANES), F32),
            pltpu.VMEM((TABLE, LANES), F32),
            pltpu.VMEM((TABLE, 2 * LANES), BF16),
            pltpu.VMEM((OWNERS, 3, 8, LANES), jnp.int32),
            pltpu.VMEM((OWNERS, 8, LANES), F32),
            pltpu.VMEM((OWNERS, LANES), jnp.int32),
            pltpu.SemaphoreType.DMA((3,)),
        ],
        name="main",
    )(
        *near(base, east, west, north, south),
        source_cells[0],
        source_weights[0],
        source_counts[0],
    )
    received = lax.all_to_all(
        partial_value, ("gx", "gy"), split_axis=0, concat_axis=0, tiled=True
    )
    obs_equiv = pl.pallas_call(
        owner_kernel,
        in_specs=[VMEM] * 2,
        out_specs=VMEM,
        out_shape=shape(OBS_DEV // LANES, LANES),
        name="owner",
    )(*near(received, slot_owner[0]))
    return smoothed.reshape(increments.shape), obs_equiv.reshape(-1)


def solution(mesh):
    return jax.shard_map(
        local,
        mesh=mesh,
        in_specs=(
            P(None, None, "gy", "gx"),
            P(None, "gy", "gx"),
            P("gy", "gx"),
            P(("gx", "gy"), None, None, None, None),
            P(("gx", "gy"), None, None, None),
            P(("gx", "gy"), None, None),
            P(("gx", "gy"), None, None),
        ),
        out_specs=(P(None, None, "gy", "gx"), P(("gx", "gy"))),
        check_vma=False,
    )
```

```python
import jax
import jax.numpy as jnp
from jax import lax
from jax.experimental import pallas as pl
from jax.experimental.pallas import tpu as pltpu
from jax.sharding import PartitionSpec as P

F32 = jnp.float32
BF16 = jnp.bfloat16
ITERS = 10
HALO = 10
OBS_DEV = 4096
LAYERS = 6
LEVELS = 3
ARRAYS = LAYERS + LEVELS
CY = 24
CX = 256
LANES = 128
STRIDE = 14
ROWS = 48
WIDE = 3
TABLE = LAYERS * CY * 2
TURN = 16
LOOKED_UP = 4
BANDS = 6
UNROLL = 5
OWNERS = 128
STAGES = 10
STRIP = (HALO * (ARRAYS + 1), CX)
VMEM = pl.BlockSpec(memory_space=pltpu.VMEM)


def iota(shape, dim):
    return lax.broadcasted_iota(jnp.int32, shape, dim)


def pack_kernel(inc_ref, dif_ref, mask_ref, base_ref, first_ref, last_ref):
    wet = mask_ref[...].astype(F32)
    lane = iota((CY, LANES), 1)
    first = jnp.zeros((CY, LANES), F32)
    last = jnp.zeros((CY, LANES), F32)
    for a in range(ARRAYS):
        values = (inc_ref[a] if a < LAYERS else dif_ref[a - LAYERS]) * wet
        base_ref[a] = values
        mine = (lane >= STRIDE * a) & (lane < STRIDE * a + HALO)
        left = values[:, :LANES]
        right = values[:, LANES:]
        if a:
            left = pltpu.roll(left, STRIDE * a, 1)
        right = pltpu.roll(right, STRIDE * a + HALO, 1)
        first = jnp.where(mine, left, first)
        last = jnp.where(mine, right, last)
    first_ref[...] = first
    last_ref[...] = last


def rows_kernel(base_ref, east_ref, west_ref, one_ref, two_ref):
    even = lax.axis_index("gy") % 2 == 0

    def fill(ref, start):
        for a in range(ARRAYS):
            ref[pl.ds(HALO * a, HALO), :] = base_ref[a, pl.ds(start, HALO), :]
        ref[pl.ds(HALO * ARRAYS, HALO), pl.ds(0, LANES)] = east_ref[pl.ds(start, HALO), :]
        ref[pl.ds(HALO * ARRAYS, HALO), pl.ds(LANES, LANES)] = west_ref[pl.ds(start, HALO), :]

    @pl.when(even)
    def _():
        fill(one_ref, CY - HALO)
        fill(two_ref, 0)

    @pl.when(jnp.logical_not(even))
    def _():
        fill(one_ref, 0)
        fill(two_ref, CY - HALO)


def plan_kernel(cells_ref, counts_ref, spots_ref, moves_ref, first_ref, second_ref, shift_ref):
    before = (iota((OWNERS, OWNERS), 1) < iota((OWNERS, OWNERS), 0)).astype(F32).astype(BF16)
    held = counts_ref[...].astype(F32).astype(BF16)
    start = jnp.dot(before, held, preferred_element_type=F32).astype(jnp.int32)
    shift_ref[...] = 8 * iota((OWNERS, LANES), 0) - start
    sub_id = iota((8, LANES), 0)
    nothing = jnp.zeros((8, LANES), jnp.int32)
    for o in range(OWNERS):
        col = cells_ref[o, 2]
        row = (col >> 7) * (LAYERS * CY) + cells_ref[o, 0] * CY + cells_ref[o, 1]
        spot = (shift_ref[pl.ds(o, 8, stride=0), :] << 16) + (row << 7) + (col & (LANES - 1))
        first_ref[o] = jnp.where(sub_id < counts_ref[pl.ds(o, 8, stride=0), :], spot, 0)
        moves_ref[o] = nothing
    old_ref, new_ref = first_ref, second_ref
    for bit in range(STAGES):
        jump = 1 << bit
        mark = 1 << (16 + bit)
        if bit == STAGES - 1:
            new_ref = spots_ref
        turned = None
        for o in range(OWNERS):
            here = old_ref[o]
            if bit >= 3:
                source = o + (jump >> 3)
                there = old_ref[source] if source < OWNERS else nothing
            else:
                if turned is None:
                    turned = pltpu.roll(here, 8 - jump, 0)
                after = pltpu.roll(old_ref[o + 1], 8 - jump, 0) if o + 1 < OWNERS else nothing
                there = jnp.where(sub_id < 8 - jump, turned, after)
                turned = after
            goes = here & mark
            moves_ref[o] = moves_ref[o] | (goes >> 16)
            new_ref[o] = jnp.where((there & mark) != 0, there, jnp.where(goes != 0, 0, here))
        old_ref, new_ref = new_ref, old_ref


def smooth(
    base_ref, east_ref, west_ref, north_ref, south_ref, out_ref, wide_ref, coeff_ref,
    table_ref,
):
    lane_tile = iota((CY, LANES), 1)
    lane_rows = iota((HALO, LANES), 1)

    def side(east, west, a, lane):
        if a:
            east = pltpu.roll(east, LANES - STRIDE * a, 1)
        west = pltpu.roll(west, (LANES - HALO - STRIDE * a) % LANES, 1)
        halo = jnp.where(lane < HALO, east, 0.0)
        return jnp.where(lane >= LANES - HALO, west, halo)

    strip = pl.ds(HALO * ARRAYS, HALO)
    for a in range(ARRAYS):
        for v in range(2):
            lanes = pl.ds(v * LANES, LANES)
            wide_ref[a, v, pl.ds(0, CY), :] = base_ref[a, :, lanes]
            wide_ref[a, v, pl.ds(CY, CY), :] = jnp.zeros((CY, LANES), F32)
            wide_ref[a, v, pl.ds(CY, HALO), :] = north_ref[pl.ds(HALO * a, HALO), lanes]
            wide_ref[a, v, pl.ds(ROWS - HALO, HALO), :] = south_ref[pl.ds(HALO * a, HALO), lanes]
        wide_ref[a, 2, pl.ds(0, CY), :] = side(east_ref[...], west_ref[...], a, lane_tile)
        wide_ref[a, 2, pl.ds(CY, CY), :] = jnp.zeros((CY, LANES), F32)
        for ref, start in ((north_ref, CY), (south_ref, ROWS - HALO)):
            wide_ref[a, 2, pl.ds(start, HALO), :] = side(
                ref[strip, pl.ds(0, LANES)], ref[strip, pl.ds(LANES, LANES)], a, lane_rows
            )

    lane = iota((8, LANES), 1)

    def bands(a):
        return [
            [wide_ref[a, v, pl.ds(b, 8, stride=BANDS), :] for v in range(WIDE)]
            for b in range(BANDS)
        ]

    def to_east(parts):
        turned = [pltpu.roll(part, LANES - 1, 1) for part in parts]
        return [
            jnp.where(lane == LANES - 1, turned[(v + 1) % WIDE], turned[v]) for v in range(WIDE)
        ]

    def to_west(parts):
        turned = [pltpu.roll(part, 1, 1) for part in parts]
        return [jnp.where(lane == 0, turned[(v - 1) % WIDE], turned[v]) for v in range(WIDE)]

    def to_north(values):
        return values[1:] + [[pltpu.roll(part, 7, 0) for part in values[0]]]

    def to_south(values):
        return [[pltpu.roll(part, 1, 0) for part in values[-1]]] + values[:-1]

    def face(here, there):
        return [
            jnp.where((x > 0.0) & (y > 0.0), 0.5 * (x + y), 0.0) for x, y in zip(here, there)
        ]

    for level in range(LEVELS):
        here = bands(LAYERS + level)
        north = [face(x, y) for x, y in zip(here, to_north(here))]
        south = to_south(north)
        for b in range(BANDS):
            east = face(here[b], to_east(here[b]))
            west = to_west(east)
            for v in range(WIDE):
                sides = (east[v], west[v], north[b][v], south[b][v])
                keep = 1.0 - ((sides[0] + sides[1]) + (sides[2] + sides[3]))
                for i, side_value in enumerate((keep,) + sides):
                    coeff_ref[level, i, b, v] = side_value

    def step(field, level):
        north = to_north(field)
        south = to_south(field)
        updated = []
        for b in range(BANDS):
            around = (field[b], to_east(field[b]), to_west(field[b]), north[b], south[b])
            parts = []
            for v in range(WIDE):
                terms = [coeff_ref[level, i, b, v] * near[v] for i, near in enumerate(around)]
                parts.append(terms[0] + ((terms[1] + terms[2]) + (terms[3] + terms[4])))
            updated.append(parts)
        return updated

    for level in range(LEVELS):

        def turn(_, fields):
            for _ in range(UNROLL):
                fields = [step(field, level) for field in fields]
            return fields

        pair = lax.fori_loop(0, ITERS // UNROLL, turn, [bands(level), bands(level + LEVELS)])
        for layer, field in zip((level, level + LEVELS), pair):
            for v in range(2):
                first = (v * LAYERS + layer) * CY
                for b in range(BANDS):
                    table_ref[pl.ds(first + b, CY // BANDS, stride=BANDS), :] = field[b][v][
                        :CY // BANDS
                    ]
                out_ref[layer, :, pl.ds(v * LANES, LANES)] = table_ref[pl.ds(first, CY), :]


def choose(parts, bits):
    turn = 0
    while len(parts) > 1:
        pairs = [
            jnp.where(bits[turn], parts[2 * j + 1], parts[2 * j]) for j in range(len(parts) // 2)
        ]
        parts = pairs + parts[2 * len(pairs):]
        turn += 1
    return parts[0]


def main_kernel(
    base_ref, east_ref, west_ref, one_ref, two_ref, spots_ref, moves_ref, weights_far, counts_far,
    smooth_ref, partial_ref, wide_ref, coeff_ref, table_ref, split_ref, north_ref, south_ref,
    first_ref, second_ref, weights_ref, counts_ref, arrived,
):
    fetches = [
        pltpu.make_async_copy(far, ref, arrived.at[i])
        for i, (far, ref) in enumerate(((weights_far, weights_ref), (counts_far, counts_ref)))
    ]
    for fetch in fetches:
        fetch.start()
    place = lax.axis_index("gy")
    even = place % 2 == 0
    edge = (place == 0) | (place == lax.axis_size("gy") - 1)
    one = one_ref[...]
    two = jnp.where(edge, 0.0, two_ref[...])
    north_ref[...] = jnp.where(even, one, two)
    south_ref[...] = jnp.where(even, two, one)
    smooth(
        base_ref, east_ref, west_ref, north_ref, south_ref, smooth_ref, wide_ref, coeff_ref,
        table_ref,
    )
    values = table_ref[...]
    coarse = values.astype(BF16)
    split_ref[:, pl.ds(0, LANES)] = coarse
    split_ref[:, pl.ds(LANES, LANES)] = (values - coarse.astype(F32)).astype(BF16)

    for fetch in fetches:
        fetch.wait()
    counts = counts_ref[...]
    rows_used = jnp.max(jnp.sum(counts.astype(F32), axis=0, keepdims=True)).astype(jnp.int32)
    groups = (rows_used + (8 * TURN - 1)) // (8 * TURN)
    split = split_ref[...]
    lane_id = iota((LANES, LANES), 0).astype(BF16)
    sub_id = iota((8, LANES), 0)

    def places(o):
        spot = spots_ref[o] & 0xFFFF
        return spot >> 7, spot & (LANES - 1)

    def by_matmul(o):
        rows_at, lane_at = places(o)
        lane_at = lane_at.astype(F32).astype(BF16)
        result = jnp.zeros((8, LANES), F32)
        for k in range(0, 8, 2):
            picks = []
            for j in (k, k + 1):
                lane_row = jnp.broadcast_to(lane_at[j:j + 1, :], (LANES, LANES))
                picks.append(jnp.where(lane_id == lane_row, BF16(1), BF16(0)))
            pick = jnp.concatenate(picks, axis=1)
            found = jnp.dot(
                split, jnp.concatenate([pick, pick], axis=0), preferred_element_type=F32
            )
            for j in (0, 1):
                block = found[:, j * LANES:(j + 1) * LANES]
                at = jnp.broadcast_to(rows_at[k + j:k + j + 1, :], (8, LANES))
                bits = [(at & (8 << b)) != 0 for b in range(6)]
                value = choose([block[8 * q:8 * q + 8] for q in range(TABLE // 8)], bits)
                value = jnp.take_along_axis(value, at & 7, axis=0)
                result = jnp.where(sub_id == k + j, value, result)
        first_ref[o] = result

    def by_lanes(owners):
        spots = [places(o) for o in owners]
        bits = [[(rows_at & (1 << b)) != 0 for b in range(3)] for rows_at, _ in spots]
        found = [jnp.zeros((8, LANES), F32) for _ in owners]
        for q in range(TABLE // 8):
            rows = [table_ref[pl.ds(8 * q + r, 8, stride=0), :] for r in range(8)]
            for i, (rows_at, lane_at) in enumerate(spots):
                value = choose([jnp.take_along_axis(row, lane_at, axis=1) for row in rows], bits[i])
                found[i] = jnp.where((rows_at >> 3) == q, value, found[i])
        for o, value in zip(owners, found):
            first_ref[o] = value

    def some(i, _):
        first = i * TURN
        for j in range(TURN - LOOKED_UP):
            by_matmul(first + j)
        for j in range(TURN - LOOKED_UP, TURN, 2):
            by_lanes((first + j, first + j + 1))
        return 0

    lax.fori_loop(0, groups, some, 0)

    old_ref, new_ref = first_ref, second_ref
    for bit in reversed(range(STAGES)):
        jump = 1 << bit
        turned = None
        for o in range(OWNERS):
            here = old_ref[o]
            if bit >= 3:
                source = o - (jump >> 3)
                there = old_ref[source] if source >= 0 else here
            else:
                now = pltpu.roll(here, jump, 0)
                there = now if turned is None else jnp.where(sub_id < jump, turned, now)
                turned = now
            new = jnp.where((moves_ref[o] & jump) != 0, there, here)
            if bit:
                new_ref[o] = new
            else:
                valid = sub_id < counts_ref[pl.ds(o, 8, stride=0), :]
                weighted = jnp.where(valid, weights_ref[o] * new, 0.0)
                partial_ref[o] = jnp.sum(weighted, axis=0, keepdims=True)
        old_ref, new_ref = new_ref, old_ref


def owner_kernel(values_ref, slots_ref, out_ref):
    high_id = iota((32, LANES), 0)
    low_id = iota((LANES, LANES), 0)
    total = jnp.zeros((64, LANES), F32)
    for g in range(0, OWNERS, 8):
        left = []
        right = []
        for j in range(g, g + 8):
            value = values_ref[j]
            slot = slots_ref[pl.ds(j, 1), :]
            coarse = value.astype(BF16).astype(F32)
            fine = value - coarse
            high = high_id == (slot >> 7)
            left.append(
                jnp.concatenate([jnp.where(high, coarse, 0.0), jnp.where(high, fine, 0.0)], axis=0)
            )
            right.append(jnp.where(low_id == (slot & 127), 1.0, 0.0))
        total = total + lax.dot_general(
            jnp.concatenate(left, axis=1).astype(BF16),
            jnp.concatenate(right, axis=1).astype(BF16),
            (((1,), (1,)), ((), ())),
            preferred_element_type=F32,
        )
    out_ref[...] = total[:32] + total[32:]


def shape(*dims):
    return jax.ShapeDtypeStruct(dims, F32)


def shift(array, axis, step):
    size = lax.axis_size(axis)
    return lax.ppermute(array, axis, [(i, (i + step) % size) for i in range(size)])


def pairs(array, axis, odd):
    size = lax.axis_size(axis)
    swaps = [(i, (((i + odd) % size) ^ 1) - odd) for i in range(size)]
    return lax.ppermute(array, axis, [(i, j % size) for i, j in swaps])


def near(*arrays):
    return [pltpu.with_memory_space_constraint(array, pltpu.MemorySpace.VMEM) for array in arrays]


def local(
    increments, diffusivity, sea_mask, source_cells, source_weights, source_counts, slot_owner
):
    base, first, last = pl.pallas_call(
        pack_kernel,
        in_specs=[VMEM] * 3,
        out_specs=(VMEM,) * 3,
        out_shape=(pltpu.VMEM((ARRAYS, CY, CX), F32),) + (pltpu.VMEM((CY, LANES), F32),) * 2,
        name="pack",
    )(increments.reshape(LAYERS, CY, CX), diffusivity, sea_mask)
    east = shift(first, "gx", -1)
    west = shift(last, "gx", 1)
    one, two = pl.pallas_call(
        rows_kernel,
        in_specs=[VMEM] * 3,
        out_specs=(VMEM,) * 2,
        out_shape=(pltpu.VMEM(STRIP, F32),) * 2,
        name="rows",
    )(*near(base, east, west))
    one = pairs(one, "gy", 0)
    two = pairs(two, "gy", 1)
    whole = pltpu.VMEM((OWNERS, 8, LANES), jnp.int32)
    spots, moves = pl.pallas_call(
        plan_kernel,
        in_specs=[VMEM] * 2,
        out_specs=(VMEM,) * 2,
        out_shape=(whole, whole),
        scratch_shapes=[whole, whole, pltpu.VMEM((OWNERS, LANES), jnp.int32)],
        name="plan",
    )(source_cells[0], source_counts[0])
    smoothed, partial_value = pl.pallas_call(
        main_kernel,
        in_specs=[VMEM] * 7 + [pl.BlockSpec(memory_space=pl.ANY)] * 2,
        out_specs=(VMEM,) * 2,
        out_shape=(shape(LAYERS, CY, CX), pltpu.VMEM((OWNERS, 1, LANES), F32)),
        scratch_shapes=[
            pltpu.VMEM((ARRAYS, WIDE, ROWS, LANES), F32),
            pltpu.VMEM((LEVELS, 5, BANDS, WIDE, 8, LANES), F32),
            pltpu.VMEM((TABLE, LANES), F32),
            pltpu.VMEM((TABLE, 2 * LANES), BF16),
            pltpu.VMEM(STRIP, F32),
            pltpu.VMEM(STRIP, F32),
            pltpu.VMEM((OWNERS, 8, LANES), F32),
            pltpu.VMEM((OWNERS, 8, LANES), F32),
            pltpu.VMEM((OWNERS, 8, LANES), F32),
            pltpu.VMEM((OWNERS, LANES), jnp.int32),
            pltpu.SemaphoreType.DMA((2,)),
        ],
        name="main",
    )(*near(base, east, west, one, two, spots, moves), source_weights[0], source_counts[0])
    received = lax.all_to_all(
        partial_value, ("gx", "gy"), split_axis=0, concat_axis=0, tiled=True
    )
    obs_equiv = pl.pallas_call(
        owner_kernel,
        in_specs=[VMEM] * 2,
        out_specs=VMEM,
        out_shape=shape(OBS_DEV // LANES, LANES),
        name="owner",
    )(*near(received, slot_owner[0]))
    return smoothed.reshape(increments.shape), obs_equiv.reshape(-1)


def solution(mesh):
    return jax.shard_map(
        local,
        mesh=mesh,
        in_specs=(
            P(None, None, "gy", "gx"),
            P(None, "gy", "gx"),
            P("gy", "gx"),
            P(("gx", "gy"), None, None, None, None),
            P(("gx", "gy"), None, None, None),
            P(("gx", "gy"), None, None),
            P(("gx", "gy"), None, None),
        ),
        out_specs=(P(None, None, "gy", "gx"), P(("gx", "gy"))),
        check_vma=False,
    )
```

```python
import jax
import jax.numpy as jnp
from jax import lax
from jax.experimental import pallas as pl
from jax.experimental.pallas import tpu as pltpu
from jax.sharding import PartitionSpec as P

F32 = jnp.float32
BF16 = jnp.bfloat16
ITERS = 10
HALO = 10
OBS_DEV = 4096
LAYERS = 6
LEVELS = 3
ARRAYS = LAYERS + LEVELS
CY = 24
CX = 256
LANES = 128
STRIDE = 14
ROWS = 48
WIDE = 3
TABLE = LAYERS * CY * 2
TURN = 16
LOOKED_UP = 5
BANDS = 6
UNROLL = 5
OWNERS = 128
STAGES = 10
STRIP = (HALO * (ARRAYS + 1), CX)
VMEM = pl.BlockSpec(memory_space=pltpu.VMEM)


def iota(shape, dim):
    return lax.broadcasted_iota(jnp.int32, shape, dim)


def pack_kernel(inc_ref, dif_ref, mask_ref, base_ref, first_ref, last_ref):
    wet = mask_ref[...].astype(F32)
    lane = iota((CY, LANES), 1)
    first = jnp.zeros((CY, LANES), F32)
    last = jnp.zeros((CY, LANES), F32)
    for a in range(ARRAYS):
        values = (inc_ref[a] if a < LAYERS else dif_ref[a - LAYERS]) * wet
        base_ref[a] = values
        mine = (lane >= STRIDE * a) & (lane < STRIDE * a + HALO)
        left = values[:, :LANES]
        right = values[:, LANES:]
        if a:
            left = pltpu.roll(left, STRIDE * a, 1)
        right = pltpu.roll(right, STRIDE * a + HALO, 1)
        first = jnp.where(mine, left, first)
        last = jnp.where(mine, right, last)
    first_ref[...] = first
    last_ref[...] = last


def rows_kernel(base_ref, east_ref, west_ref, one_ref, two_ref):
    even = lax.axis_index("gy") % 2 == 0

    def fill(ref, start):
        for a in range(ARRAYS):
            ref[pl.ds(HALO * a, HALO), :] = base_ref[a, pl.ds(start, HALO), :]
        ref[pl.ds(HALO * ARRAYS, HALO), pl.ds(0, LANES)] = east_ref[pl.ds(start, HALO), :]
        ref[pl.ds(HALO * ARRAYS, HALO), pl.ds(LANES, LANES)] = west_ref[pl.ds(start, HALO), :]

    @pl.when(even)
    def _():
        fill(one_ref, CY - HALO)
        fill(two_ref, 0)

    @pl.when(jnp.logical_not(even))
    def _():
        fill(one_ref, 0)
        fill(two_ref, CY - HALO)


def plan_kernel(cells_ref, counts_ref, spots_ref, moves_ref, first_ref, second_ref, shift_ref):
    before = (iota((OWNERS, OWNERS), 1) < iota((OWNERS, OWNERS), 0)).astype(F32).astype(BF16)
    held = counts_ref[...].astype(F32).astype(BF16)
    start = jnp.dot(before, held, preferred_element_type=F32).astype(jnp.int32)
    shift_ref[...] = 8 * iota((OWNERS, LANES), 0) - start
    sub_id = iota((8, LANES), 0)
    nothing = jnp.zeros((8, LANES), jnp.int32)
    for o in range(OWNERS):
        col = cells_ref[o, 2]
        row = (col >> 7) * (LAYERS * CY) + cells_ref[o, 0] * CY + cells_ref[o, 1]
        spot = (shift_ref[pl.ds(o, 8, stride=0), :] << 16) + (row << 7) + (col & (LANES - 1))
        first_ref[o] = jnp.where(sub_id < counts_ref[pl.ds(o, 8, stride=0), :], spot, 0)
        moves_ref[o] = nothing
    old_ref, new_ref = first_ref, second_ref
    for bit in range(STAGES):
        jump = 1 << bit
        mark = 1 << (16 + bit)
        if bit == STAGES - 1:
            new_ref = spots_ref
        turned = None
        for o in range(OWNERS):
            here = old_ref[o]
            if bit >= 3:
                source = o + (jump >> 3)
                there = old_ref[source] if source < OWNERS else nothing
            else:
                if turned is None:
                    turned = pltpu.roll(here, 8 - jump, 0)
                after = pltpu.roll(old_ref[o + 1], 8 - jump, 0) if o + 1 < OWNERS else nothing
                there = jnp.where(sub_id < 8 - jump, turned, after)
                turned = after
            goes = here & mark
            moves_ref[o] = moves_ref[o] | (goes >> 16)
            new_ref[o] = jnp.where((there & mark) != 0, there, jnp.where(goes != 0, 0, here))
        old_ref, new_ref = new_ref, old_ref


def smooth(
    base_ref, east_ref, west_ref, north_ref, south_ref, out_ref, wide_ref, coeff_ref,
    table_ref,
):
    lane_tile = iota((CY, LANES), 1)
    lane_rows = iota((HALO, LANES), 1)

    def side(east, west, a, lane):
        if a:
            east = pltpu.roll(east, LANES - STRIDE * a, 1)
        west = pltpu.roll(west, (LANES - HALO - STRIDE * a) % LANES, 1)
        halo = jnp.where(lane < HALO, east, 0.0)
        return jnp.where(lane >= LANES - HALO, west, halo)

    strip = pl.ds(HALO * ARRAYS, HALO)
    for a in range(ARRAYS):
        for v in range(2):
            lanes = pl.ds(v * LANES, LANES)
            wide_ref[a, v, pl.ds(0, CY), :] = base_ref[a, :, lanes]
            wide_ref[a, v, pl.ds(CY, CY), :] = jnp.zeros((CY, LANES), F32)
            wide_ref[a, v, pl.ds(CY, HALO), :] = north_ref[pl.ds(HALO * a, HALO), lanes]
            wide_ref[a, v, pl.ds(ROWS - HALO, HALO), :] = south_ref[pl.ds(HALO * a, HALO), lanes]
        wide_ref[a, 2, pl.ds(0, CY), :] = side(east_ref[...], west_ref[...], a, lane_tile)
        wide_ref[a, 2, pl.ds(CY, CY), :] = jnp.zeros((CY, LANES), F32)
        for ref, start in ((north_ref, CY), (south_ref, ROWS - HALO)):
            wide_ref[a, 2, pl.ds(start, HALO), :] = side(
                ref[strip, pl.ds(0, LANES)], ref[strip, pl.ds(LANES, LANES)], a, lane_rows
            )

    lane = iota((8, LANES), 1)

    def bands(a):
        return [
            [wide_ref[a, v, pl.ds(b, 8, stride=BANDS), :] for v in range(WIDE)]
            for b in range(BANDS)
        ]

    def to_east(parts):
        turned = [pltpu.roll(part, LANES - 1, 1) for part in parts]
        return [
            jnp.where(lane == LANES - 1, turned[(v + 1) % WIDE], turned[v]) for v in range(WIDE)
        ]

    def to_west(parts):
        turned = [pltpu.roll(part, 1, 1) for part in parts]
        return [jnp.where(lane == 0, turned[(v - 1) % WIDE], turned[v]) for v in range(WIDE)]

    def to_north(values):
        return values[1:] + [[pltpu.roll(part, 7, 0) for part in values[0]]]

    def to_south(values):
        return [[pltpu.roll(part, 1, 0) for part in values[-1]]] + values[:-1]

    def face(here, there):
        return [
            jnp.where((x > 0.0) & (y > 0.0), 0.5 * (x + y), 0.0) for x, y in zip(here, there)
        ]

    for level in range(LEVELS):
        here = bands(LAYERS + level)
        north = [face(x, y) for x, y in zip(here, to_north(here))]
        south = to_south(north)
        for b in range(BANDS):
            east = face(here[b], to_east(here[b]))
            west = to_west(east)
            for v in range(WIDE):
                sides = (east[v], west[v], north[b][v], south[b][v])
                keep = 1.0 - ((sides[0] + sides[1]) + (sides[2] + sides[3]))
                for i, side_value in enumerate((keep,) + sides):
                    coeff_ref[level, i, b, v] = side_value

    def step(field, level):
        north = to_north(field)
        south = to_south(field)
        updated = []
        for b in range(BANDS):
            around = (field[b], to_east(field[b]), to_west(field[b]), north[b], south[b])
            parts = []
            for v in range(WIDE):
                terms = [coeff_ref[level, i, b, v] * near[v] for i, near in enumerate(around)]
                parts.append(terms[0] + ((terms[1] + terms[2]) + (terms[3] + terms[4])))
            updated.append(parts)
        return updated

    for level in range(LEVELS):

        def turn(_, fields):
            for _ in range(UNROLL):
                fields = [step(field, level) for field in fields]
            return fields

        pair = lax.fori_loop(0, ITERS // UNROLL, turn, [bands(level), bands(level + LEVELS)])
        for layer, field in zip((level, level + LEVELS), pair):
            for v in range(2):
                first = (v * LAYERS + layer) * CY
                for b in range(BANDS):
                    table_ref[pl.ds(first + b, CY // BANDS, stride=BANDS), :] = field[b][v][
                        :CY // BANDS
                    ]
                out_ref[layer, :, pl.ds(v * LANES, LANES)] = table_ref[pl.ds(first, CY), :]


def choose(parts, bits):
    turn = 0
    while len(parts) > 1:
        pairs = [
            jnp.where(bits[turn], parts[2 * j + 1], parts[2 * j]) for j in range(len(parts) // 2)
        ]
        parts = pairs + parts[2 * len(pairs):]
        turn += 1
    return parts[0]


def main_kernel(
    base_ref, east_ref, west_ref, one_ref, two_ref, spots_ref, moves_ref, weights_far, counts_far,
    smooth_far, partial_ref, wide_ref, coeff_ref, table_ref, split_ref, north_ref, south_ref,
    first_ref, second_ref, weights_ref, counts_ref, smooth_ref, arrived,
):
    fetches = [
        pltpu.make_async_copy(far, ref, arrived.at[i])
        for i, (far, ref) in enumerate(((weights_far, weights_ref), (counts_far, counts_ref)))
    ]
    for fetch in fetches:
        fetch.start()
    place = lax.axis_index("gy")
    even = place % 2 == 0
    edge = (place == 0) | (place == lax.axis_size("gy") - 1)
    one = one_ref[...]
    two = jnp.where(edge, 0.0, two_ref[...])
    north_ref[...] = jnp.where(even, one, two)
    south_ref[...] = jnp.where(even, two, one)
    smooth(
        base_ref, east_ref, west_ref, north_ref, south_ref, smooth_ref, wide_ref, coeff_ref,
        table_ref,
    )
    leave = pltpu.make_async_copy(smooth_ref, smooth_far, arrived.at[2])
    leave.start()
    values = table_ref[...]
    coarse = values.astype(BF16)
    split_ref[:, pl.ds(0, LANES)] = coarse
    split_ref[:, pl.ds(LANES, LANES)] = (values - coarse.astype(F32)).astype(BF16)

    for fetch in fetches:
        fetch.wait()
    counts = counts_ref[...]
    rows_used = jnp.max(jnp.sum(counts.astype(F32), axis=0, keepdims=True)).astype(jnp.int32)
    groups = (rows_used + (8 * TURN - 1)) // (8 * TURN)
    split = split_ref[...]
    lane_id = iota((LANES, LANES), 0).astype(BF16)
    sub_id = iota((8, LANES), 0)

    def places(o):
        spot = spots_ref[o] & 0xFFFF
        return spot >> 7, spot & (LANES - 1)

    def by_matmul(o):
        rows_at, lane_at = places(o)
        lane_at = lane_at.astype(F32).astype(BF16)
        result = jnp.zeros((8, LANES), F32)
        for k in range(0, 8, 2):
            picks = []
            for j in (k, k + 1):
                lane_row = jnp.broadcast_to(lane_at[j:j + 1, :], (LANES, LANES))
                picks.append(jnp.where(lane_id == lane_row, BF16(1), BF16(0)))
            pick = jnp.concatenate(picks, axis=1)
            found = jnp.dot(
                split, jnp.concatenate([pick, pick], axis=0), preferred_element_type=F32
            )
            for j in (0, 1):
                block = found[:, j * LANES:(j + 1) * LANES]
                at = jnp.broadcast_to(rows_at[k + j:k + j + 1, :], (8, LANES))
                bits = [(at & (8 << b)) != 0 for b in range(6)]
                value = choose([block[8 * q:8 * q + 8] for q in range(TABLE // 8)], bits)
                value = jnp.take_along_axis(value, at & 7, axis=0)
                result = jnp.where(sub_id == k + j, value, result)
        first_ref[o] = result

    def by_lanes(o):
        rows_at, lane_at = places(o)
        bits = [(rows_at & (1 << b)) != 0 for b in range(3)]
        found = jnp.zeros((8, LANES), F32)
        for q in range(TABLE // 8):
            rows = [table_ref[pl.ds(8 * q + r, 8, stride=0), :] for r in range(8)]
            value = choose([jnp.take_along_axis(row, lane_at, axis=1) for row in rows], bits)
            found = jnp.where((rows_at >> 3) == q, value, found)
        first_ref[o] = found

    def some(i, _):
        first = i * TURN
        for j in range(TURN - LOOKED_UP):
            by_matmul(first + j)
        for j in range(TURN - LOOKED_UP, TURN):
            by_lanes(first + j)
        return 0

    lax.fori_loop(0, groups, some, 0)

    old_ref, new_ref = first_ref, second_ref
    for bit in reversed(range(STAGES)):
        jump = 1 << bit
        turned = None
        for o in range(OWNERS):
            here = old_ref[o]
            if bit >= 3:
                source = o - (jump >> 3)
                there = old_ref[source] if source >= 0 else here
            else:
                now = pltpu.roll(here, jump, 0)
                there = now if turned is None else jnp.where(sub_id < jump, turned, now)
                turned = now
            new = jnp.where((moves_ref[o] & jump) != 0, there, here)
            if bit:
                new_ref[o] = new
            else:
                valid = sub_id < counts_ref[pl.ds(o, 8, stride=0), :]
                weighted = jnp.where(valid, weights_ref[o] * new, 0.0)
                partial_ref[o] = jnp.sum(weighted, axis=0, keepdims=True)
        old_ref, new_ref = new_ref, old_ref
    leave.wait()


def owner_kernel(values_ref, slots_ref, out_ref):
    high_id = iota((32, LANES), 0).astype(BF16)
    low_id = iota((LANES, LANES), 0).astype(BF16)
    slots = slots_ref[...]
    highs = (slots >> 7).astype(F32).astype(BF16)
    lows = (slots & (LANES - 1)).astype(F32).astype(BF16)
    none = jnp.zeros((32, LANES), BF16)
    total = jnp.zeros((LANES, 64), F32)
    for g in range(0, OWNERS, 8):
        left = []
        right = []
        for j in range(g, g + 8):
            value = values_ref[j]
            coarse = value.astype(BF16)
            fine = (value - coarse.astype(F32)).astype(BF16)
            high = high_id == jnp.broadcast_to(highs[j:j + 1, :], (32, LANES))
            low = low_id == jnp.broadcast_to(lows[j:j + 1, :], (LANES, LANES))
            parts = [
                jnp.where(high, jnp.broadcast_to(part, (32, LANES)), none)
                for part in (coarse, fine)
            ]
            right.append(jnp.concatenate(parts, axis=0))
            left.append(jnp.where(low, BF16(1), BF16(0)))
        total = total + lax.dot_general(
            jnp.concatenate(left, axis=1),
            jnp.concatenate(right, axis=1),
            (((1,), (1,)), ((), ())),
            preferred_element_type=F32,
        )
    total = total.T
    out_ref[...] = total[:32] + total[32:]


def shape(*dims):
    return jax.ShapeDtypeStruct(dims, F32)


def shift(array, axis, step):
    size = lax.axis_size(axis)
    return lax.ppermute(array, axis, [(i, (i + step) % size) for i in range(size)])


def pairs(array, axis, odd):
    size = lax.axis_size(axis)
    swaps = [(i, (((i + odd) % size) ^ 1) - odd) for i in range(size)]
    return lax.ppermute(array, axis, [(i, j % size) for i, j in swaps])


def near(*arrays):
    return [pltpu.with_memory_space_constraint(array, pltpu.MemorySpace.VMEM) for array in arrays]


def local(
    increments, diffusivity, sea_mask, source_cells, source_weights, source_counts, slot_owner
):
    base, first, last = pl.pallas_call(
        pack_kernel,
        in_specs=[VMEM] * 3,
        out_specs=(VMEM,) * 3,
        out_shape=(pltpu.VMEM((ARRAYS, CY, CX), F32),) + (pltpu.VMEM((CY, LANES), F32),) * 2,
        name="pack",
    )(increments.reshape(LAYERS, CY, CX), diffusivity, sea_mask)
    east = shift(first, "gx", -1)
    west = shift(last, "gx", 1)
    one, two = pl.pallas_call(
        rows_kernel,
        in_specs=[VMEM] * 3,
        out_specs=(VMEM,) * 2,
        out_shape=(pltpu.VMEM(STRIP, F32),) * 2,
        name="rows",
    )(*near(base, east, west))
    one = pairs(one, "gy", 0)
    two = pairs(two, "gy", 1)
    whole = pltpu.VMEM((OWNERS, 8, LANES), jnp.int32)
    spots, moves = pl.pallas_call(
        plan_kernel,
        in_specs=[VMEM] * 2,
        out_specs=(VMEM,) * 2,
        out_shape=(whole, whole),
        scratch_shapes=[whole, whole, pltpu.VMEM((OWNERS, LANES), jnp.int32)],
        name="plan",
    )(source_cells[0], source_counts[0])
    smoothed, partial_value = pl.pallas_call(
        main_kernel,
        in_specs=[VMEM] * 7 + [pl.BlockSpec(memory_space=pl.ANY)] * 2,
        out_specs=(pl.BlockSpec(memory_space=pl.ANY), VMEM),
        out_shape=(shape(LAYERS, CY, CX), pltpu.VMEM((OWNERS, 1, LANES), F32)),
        scratch_shapes=[
            pltpu.VMEM((ARRAYS, WIDE, ROWS, LANES), F32),
            pltpu.VMEM((LEVELS, 5, BANDS, WIDE, 8, LANES), F32),
            pltpu.VMEM((TABLE, LANES), F32),
            pltpu.VMEM((TABLE, 2 * LANES), BF16),
            pltpu.VMEM(STRIP, F32),
            pltpu.VMEM(STRIP, F32),
            pltpu.VMEM((OWNERS, 8, LANES), F32),
            pltpu.VMEM((OWNERS, 8, LANES), F32),
            pltpu.VMEM((OWNERS, 8, LANES), F32),
            pltpu.VMEM((OWNERS, LANES), jnp.int32),
            pltpu.VMEM((LAYERS, CY, CX), F32),
            pltpu.SemaphoreType.DMA((3,)),
        ],
        name="main",
    )(*near(base, east, west, one, two, spots, moves), source_weights[0], source_counts[0])
    received = lax.all_to_all(
        partial_value, ("gx", "gy"), split_axis=0, concat_axis=0, tiled=True
    )
    obs_equiv = pl.pallas_call(
        owner_kernel,
        in_specs=[VMEM] * 2,
        out_specs=VMEM,
        out_shape=shape(OBS_DEV // LANES, LANES),
        name="owner",
    )(*near(received, slot_owner[0]))
    return smoothed.reshape(increments.shape), obs_equiv.reshape(-1)


def solution(mesh):
    return jax.shard_map(
        local,
        mesh=mesh,
        in_specs=(
            P(None, None, "gy", "gx"),
            P(None, "gy", "gx"),
            P("gy", "gx"),
            P(("gx", "gy"), None, None, None, None),
            P(("gx", "gy"), None, None, None),
            P(("gx", "gy"), None, None),
            P(("gx", "gy"), None, None),
        ),
        out_specs=(P(None, None, "gy", "gx"), P(("gx", "gy"))),
        check_vma=False,
    )
```

```python
import jax
import jax.numpy as jnp
from jax import lax
from jax.experimental import pallas as pl
from jax.experimental.pallas import tpu as pltpu
from jax.sharding import PartitionSpec as P

F32 = jnp.float32
BF16 = jnp.bfloat16
ITERS = 10
HALO = 10
OBS_DEV = 4096
LAYERS = 6
LEVELS = 3
ARRAYS = LAYERS + LEVELS
CY = 24
CX = 256
LANES = 128
STRIDE = 14
ROWS = 48
WIDE = 3
TABLE = LAYERS * CY * 2
MOST = 40
TURN = 16
LOOKED_UP = 5
BANDS = 6
UNROLL = 5
OWNERS = 128
STAGES = 10
STRIP = (HALO * (ARRAYS + 1), CX)
VMEM = pl.BlockSpec(memory_space=pltpu.VMEM)


def iota(shape, dim):
    return lax.broadcasted_iota(jnp.int32, shape, dim)


def pack_kernel(inc_ref, dif_ref, mask_ref, base_ref, first_ref, last_ref):
    wet = mask_ref[...].astype(F32)
    lane = iota((CY, LANES), 1)
    first = jnp.zeros((CY, LANES), F32)
    last = jnp.zeros((CY, LANES), F32)
    for a in range(ARRAYS):
        values = (inc_ref[a] if a < LAYERS else dif_ref[a - LAYERS]) * wet
        base_ref[a] = values
        mine = (lane >= STRIDE * a) & (lane < STRIDE * a + HALO)
        left = values[:, :LANES]
        right = values[:, LANES:]
        if a:
            left = pltpu.roll(left, STRIDE * a, 1)
        right = pltpu.roll(right, STRIDE * a + HALO, 1)
        first = jnp.where(mine, left, first)
        last = jnp.where(mine, right, last)
    first_ref[...] = first
    last_ref[...] = last


def rows_kernel(base_ref, east_ref, west_ref, one_ref, two_ref):
    even = lax.axis_index("gy") % 2 == 0

    def fill(ref, start):
        for a in range(ARRAYS):
            ref[pl.ds(HALO * a, HALO), :] = base_ref[a, pl.ds(start, HALO), :]
        ref[pl.ds(HALO * ARRAYS, HALO), pl.ds(0, LANES)] = east_ref[pl.ds(start, HALO), :]
        ref[pl.ds(HALO * ARRAYS, HALO), pl.ds(LANES, LANES)] = west_ref[pl.ds(start, HALO), :]

    @pl.when(even)
    def _():
        fill(one_ref, CY - HALO)
        fill(two_ref, 0)

    @pl.when(jnp.logical_not(even))
    def _():
        fill(one_ref, 0)
        fill(two_ref, CY - HALO)


def plan_kernel(cells_ref, counts_ref, spots_ref, moves_ref, first_ref, second_ref, shift_ref):
    before = (iota((OWNERS, OWNERS), 1) < iota((OWNERS, OWNERS), 0)).astype(F32).astype(BF16)
    held = counts_ref[...].astype(F32).astype(BF16)
    start = jnp.dot(before, held, preferred_element_type=F32).astype(jnp.int32)
    shift_ref[...] = 8 * iota((OWNERS, LANES), 0) - start
    sub_id = iota((8, LANES), 0)
    nothing = jnp.zeros((8, LANES), jnp.int32)
    for o in range(OWNERS):
        col = cells_ref[o, 2]
        row = (col >> 7) * (LAYERS * CY) + cells_ref[o, 0] * CY + cells_ref[o, 1]
        spot = (shift_ref[pl.ds(o, 8, stride=0), :] << 16) + (row << 7) + (col & (LANES - 1))
        first_ref[o] = jnp.where(sub_id < counts_ref[pl.ds(o, 8, stride=0), :], spot, 0)
        moves_ref[o] = nothing
    old_ref, new_ref = first_ref, second_ref
    for bit in range(STAGES):
        jump = 1 << bit
        mark = 1 << (16 + bit)
        if bit == STAGES - 1:
            new_ref = spots_ref
        turned = None
        for o in range(OWNERS):
            here = old_ref[o]
            if bit >= 3:
                source = o + (jump >> 3)
                there = old_ref[source] if source < OWNERS else nothing
            else:
                if turned is None:
                    turned = pltpu.roll(here, 8 - jump, 0)
                after = pltpu.roll(old_ref[o + 1], 8 - jump, 0) if o + 1 < OWNERS else nothing
                there = jnp.where(sub_id < 8 - jump, turned, after)
                turned = after
            goes = here & mark
            moves_ref[o] = moves_ref[o] | (goes >> 16)
            new_ref[o] = jnp.where((there & mark) != 0, there, jnp.where(goes != 0, 0, here))
        old_ref, new_ref = new_ref, old_ref


def smooth(
    base_ref, east_ref, west_ref, north_ref, south_ref, out_ref, wide_ref, coeff_ref,
    table_ref,
):
    lane_tile = iota((CY, LANES), 1)
    lane_rows = iota((HALO, LANES), 1)

    def side(east, west, a, lane):
        if a:
            east = pltpu.roll(east, LANES - STRIDE * a, 1)
        west = pltpu.roll(west, (LANES - HALO - STRIDE * a) % LANES, 1)
        halo = jnp.where(lane < HALO, east, 0.0)
        return jnp.where(lane >= LANES - HALO, west, halo)

    strip = pl.ds(HALO * ARRAYS, HALO)
    for a in range(ARRAYS):
        for v in range(2):
            lanes = pl.ds(v * LANES, LANES)
            wide_ref[a, v, pl.ds(0, CY), :] = base_ref[a, :, lanes]
            wide_ref[a, v, pl.ds(CY, CY), :] = jnp.zeros((CY, LANES), F32)
            wide_ref[a, v, pl.ds(CY, HALO), :] = north_ref[pl.ds(HALO * a, HALO), lanes]
            wide_ref[a, v, pl.ds(ROWS - HALO, HALO), :] = south_ref[pl.ds(HALO * a, HALO), lanes]
        wide_ref[a, 2, pl.ds(0, CY), :] = side(east_ref[...], west_ref[...], a, lane_tile)
        wide_ref[a, 2, pl.ds(CY, CY), :] = jnp.zeros((CY, LANES), F32)
        for ref, start in ((north_ref, CY), (south_ref, ROWS - HALO)):
            wide_ref[a, 2, pl.ds(start, HALO), :] = side(
                ref[strip, pl.ds(0, LANES)], ref[strip, pl.ds(LANES, LANES)], a, lane_rows
            )

    lane = iota((8, LANES), 1)

    def bands(a):
        return [
            [wide_ref[a, v, pl.ds(b, 8, stride=BANDS), :] for v in range(WIDE)]
            for b in range(BANDS)
        ]

    def to_east(parts):
        turned = [pltpu.roll(part, LANES - 1, 1) for part in parts]
        return [
            jnp.where(lane == LANES - 1, turned[(v + 1) % WIDE], turned[v]) for v in range(WIDE)
        ]

    def to_west(parts):
        turned = [pltpu.roll(part, 1, 1) for part in parts]
        return [jnp.where(lane == 0, turned[(v - 1) % WIDE], turned[v]) for v in range(WIDE)]

    def to_north(values):
        return values[1:] + [[pltpu.roll(part, 7, 0) for part in values[0]]]

    def to_south(values):
        return [[pltpu.roll(part, 1, 0) for part in values[-1]]] + values[:-1]

    def face(here, there):
        return [
            jnp.where((x > 0.0) & (y > 0.0), 0.5 * (x + y), 0.0) for x, y in zip(here, there)
        ]

    for level in range(LEVELS):
        here = bands(LAYERS + level)
        north = [face(x, y) for x, y in zip(here, to_north(here))]
        south = to_south(north)
        for b in range(BANDS):
            east = face(here[b], to_east(here[b]))
            west = to_west(east)
            for v in range(WIDE):
                sides = (east[v], west[v], north[b][v], south[b][v])
                keep = 1.0 - ((sides[0] + sides[1]) + (sides[2] + sides[3]))
                for i, side_value in enumerate((keep,) + sides):
                    coeff_ref[level, i, b, v] = side_value

    def step(field, level):
        north = to_north(field)
        south = to_south(field)
        updated = []
        for b in range(BANDS):
            around = (field[b], to_east(field[b]), to_west(field[b]), north[b], south[b])
            parts = []
            for v in range(WIDE):
                terms = [coeff_ref[level, i, b, v] * near[v] for i, near in enumerate(around)]
                parts.append(terms[0] + ((terms[1] + terms[2]) + (terms[3] + terms[4])))
            updated.append(parts)
        return updated

    for level in range(LEVELS):

        def turn(_, fields):
            for _ in range(UNROLL):
                fields = [step(field, level) for field in fields]
            return fields

        pair = lax.fori_loop(0, ITERS // UNROLL, turn, [bands(level), bands(level + LEVELS)])
        for layer, field in zip((level, level + LEVELS), pair):
            for v in range(2):
                first = (v * LAYERS + layer) * CY
                for b in range(BANDS):
                    table_ref[pl.ds(first + b, CY // BANDS, stride=BANDS), :] = field[b][v][
                        :CY // BANDS
                    ]
                out_ref[layer, :, pl.ds(v * LANES, LANES)] = table_ref[pl.ds(first, CY), :]


def choose(parts, bits):
    turn = 0
    while len(parts) > 1:
        pairs = [
            jnp.where(bits[turn], parts[2 * j + 1], parts[2 * j]) for j in range(len(parts) // 2)
        ]
        parts = pairs + parts[2 * len(pairs):]
        turn += 1
    return parts[0]


def main_kernel(
    base_ref, east_ref, west_ref, one_ref, two_ref, spots_ref, moves_ref, weights_far, counts_far,
    smooth_far, partial_ref, wide_ref, coeff_ref, table_ref, split_ref, north_ref, south_ref,
    first_ref, second_ref, weights_ref, counts_ref, smooth_ref, arrived,
):
    fetches = [
        pltpu.make_async_copy(far, ref, arrived.at[i])
        for i, (far, ref) in enumerate(((weights_far, weights_ref), (counts_far, counts_ref)))
    ]
    for fetch in fetches:
        fetch.start()
    place = lax.axis_index("gy")
    even = place % 2 == 0
    edge = (place == 0) | (place == lax.axis_size("gy") - 1)
    one = one_ref[...]
    two = jnp.where(edge, 0.0, two_ref[...])
    north_ref[...] = jnp.where(even, one, two)
    south_ref[...] = jnp.where(even, two, one)
    smooth(
        base_ref, east_ref, west_ref, north_ref, south_ref, smooth_ref, wide_ref, coeff_ref,
        table_ref,
    )
    leave = pltpu.make_async_copy(smooth_ref, smooth_far, arrived.at[2])
    leave.start()
    values = table_ref[...]
    coarse = values.astype(BF16)
    split_ref[:, pl.ds(0, LANES)] = coarse
    split_ref[:, pl.ds(LANES, LANES)] = (values - coarse.astype(F32)).astype(BF16)

    for fetch in fetches:
        fetch.wait()
    counts = counts_ref[...]
    rows_used = jnp.max(jnp.sum(counts.astype(F32), axis=0, keepdims=True)).astype(jnp.int32)
    split = split_ref[...]
    lane_id = iota((LANES, LANES), 0).astype(BF16)
    sub_id = iota((8, LANES), 0)

    def places(o):
        spot = spots_ref[o] & 0xFFFF
        return spot >> 7, spot & (LANES - 1)

    def by_matmul(o):
        rows_at, lane_at = places(o)
        lane_at = lane_at.astype(F32).astype(BF16)
        result = jnp.zeros((8, LANES), F32)
        for k in range(0, 8, 2):
            picks = []
            for j in (k, k + 1):
                lane_row = jnp.broadcast_to(lane_at[j:j + 1, :], (LANES, LANES))
                picks.append(jnp.where(lane_id == lane_row, BF16(1), BF16(0)))
            pick = jnp.concatenate(picks, axis=1)
            found = jnp.dot(
                split, jnp.concatenate([pick, pick], axis=0), preferred_element_type=F32
            )
            for j in (0, 1):
                block = found[:, j * LANES:(j + 1) * LANES]
                at = jnp.broadcast_to(rows_at[k + j:k + j + 1, :], (8, LANES))
                bits = [(at & (8 << b)) != 0 for b in range(6)]
                value = choose([block[8 * q:8 * q + 8] for q in range(TABLE // 8)], bits)
                value = jnp.take_along_axis(value, at & 7, axis=0)
                result = jnp.where(sub_id == k + j, value, result)
        first_ref[o] = result

    def by_lanes(o):
        rows_at, lane_at = places(o)
        bits = [(rows_at & (1 << b)) != 0 for b in range(3)]
        found = jnp.zeros((8, LANES), F32)
        for q in range(TABLE // 8):
            rows = [table_ref[pl.ds(8 * q + r, 8, stride=0), :] for r in range(8)]
            value = choose([jnp.take_along_axis(row, lane_at, axis=1) for row in rows], bits)
            found = jnp.where((rows_at >> 3) == q, value, found)
        first_ref[o] = found

    def lookup(first, size, singles):
        for j in range(size - singles):
            by_matmul(first + j)
        for j in range(size - singles, size):
            by_lanes(first + j)

    def most(i, _):
        lookup(i * MOST, MOST, 13)
        return 0

    def rest(i, _):
        lookup(2 * MOST + i * TURN, TURN, LOOKED_UP)
        return 0

    lax.fori_loop(0, jnp.minimum((rows_used + (8 * MOST - 1)) // (8 * MOST), 2), most, 0)
    left = jnp.maximum(rows_used - 16 * MOST, 0)
    lax.fori_loop(0, (left + (8 * TURN - 1)) // (8 * TURN), rest, 0)

    old_ref, new_ref = first_ref, second_ref
    for bit in reversed(range(STAGES)):
        jump = 1 << bit
        turned = None
        for o in range(OWNERS):
            here = old_ref[o]
            if bit >= 3:
                source = o - (jump >> 3)
                there = old_ref[source] if source >= 0 else here
            else:
                now = pltpu.roll(here, jump, 0)
                there = now if turned is None else jnp.where(sub_id < jump, turned, now)
                turned = now
            new = jnp.where((moves_ref[o] & jump) != 0, there, here)
            if bit:
                new_ref[o] = new
            else:
                valid = sub_id < counts_ref[pl.ds(o, 8, stride=0), :]
                weighted = jnp.where(valid, weights_ref[o] * new, 0.0)
                partial_ref[o] = jnp.sum(weighted, axis=0, keepdims=True)
        old_ref, new_ref = new_ref, old_ref
    leave.wait()


def owner_kernel(values_ref, slots_ref, out_ref):
    high_id = iota((32, LANES), 0).astype(BF16)
    low_id = iota((LANES, LANES), 0).astype(BF16)
    slots = slots_ref[...]
    highs = (slots >> 7).astype(F32).astype(BF16)
    lows = (slots & (LANES - 1)).astype(F32).astype(BF16)
    none = jnp.zeros((32, LANES), BF16)
    total = jnp.zeros((LANES, 64), F32)
    for g in range(0, OWNERS, 8):
        left = []
        right = []
        for j in range(g, g + 8):
            value = values_ref[j]
            coarse = value.astype(BF16)
            fine = (value - coarse.astype(F32)).astype(BF16)
            high = high_id == jnp.broadcast_to(highs[j:j + 1, :], (32, LANES))
            low = low_id == jnp.broadcast_to(lows[j:j + 1, :], (LANES, LANES))
            parts = [
                jnp.where(high, jnp.broadcast_to(part, (32, LANES)), none)
                for part in (coarse, fine)
            ]
            right.append(jnp.concatenate(parts, axis=0))
            left.append(jnp.where(low, BF16(1), BF16(0)))
        total = total + lax.dot_general(
            jnp.concatenate(left, axis=1),
            jnp.concatenate(right, axis=1),
            (((1,), (1,)), ((), ())),
            preferred_element_type=F32,
        )
    total = total.T
    out_ref[...] = total[:32] + total[32:]


def shape(*dims):
    return jax.ShapeDtypeStruct(dims, F32)


def shift(array, axis, step):
    size = lax.axis_size(axis)
    return lax.ppermute(array, axis, [(i, (i + step) % size) for i in range(size)])


def pairs(array, axis, odd):
    size = lax.axis_size(axis)
    swaps = [(i, (((i + odd) % size) ^ 1) - odd) for i in range(size)]
    return lax.ppermute(array, axis, [(i, j % size) for i, j in swaps])


def near(*arrays):
    return [pltpu.with_memory_space_constraint(array, pltpu.MemorySpace.VMEM) for array in arrays]


def local(
    increments, diffusivity, sea_mask, source_cells, source_weights, source_counts, slot_owner
):
    base, first, last = pl.pallas_call(
        pack_kernel,
        in_specs=[VMEM] * 3,
        out_specs=(VMEM,) * 3,
        out_shape=(pltpu.VMEM((ARRAYS, CY, CX), F32),) + (pltpu.VMEM((CY, LANES), F32),) * 2,
        name="pack",
    )(increments.reshape(LAYERS, CY, CX), diffusivity, sea_mask)
    east = shift(first, "gx", -1)
    west = shift(last, "gx", 1)
    one, two = pl.pallas_call(
        rows_kernel,
        in_specs=[VMEM] * 3,
        out_specs=(VMEM,) * 2,
        out_shape=(pltpu.VMEM(STRIP, F32),) * 2,
        name="rows",
    )(*near(base, east, west))
    one = pairs(one, "gy", 0)
    two = pairs(two, "gy", 1)
    whole = pltpu.VMEM((OWNERS, 8, LANES), jnp.int32)
    spots, moves = pl.pallas_call(
        plan_kernel,
        in_specs=[VMEM] * 2,
        out_specs=(VMEM,) * 2,
        out_shape=(whole, whole),
        scratch_shapes=[whole, whole, pltpu.VMEM((OWNERS, LANES), jnp.int32)],
        name="plan",
    )(source_cells[0], source_counts[0])
    smoothed, partial_value = pl.pallas_call(
        main_kernel,
        in_specs=[VMEM] * 7 + [pl.BlockSpec(memory_space=pl.ANY)] * 2,
        out_specs=(pl.BlockSpec(memory_space=pl.ANY), VMEM),
        out_shape=(shape(LAYERS, CY, CX), pltpu.VMEM((OWNERS, 1, LANES), F32)),
        scratch_shapes=[
            pltpu.VMEM((ARRAYS, WIDE, ROWS, LANES), F32),
            pltpu.VMEM((LEVELS, 5, BANDS, WIDE, 8, LANES), F32),
            pltpu.VMEM((TABLE, LANES), F32),
            pltpu.VMEM((TABLE, 2 * LANES), BF16),
            pltpu.VMEM(STRIP, F32),
            pltpu.VMEM(STRIP, F32),
            pltpu.VMEM((OWNERS, 8, LANES), F32),
            pltpu.VMEM((OWNERS, 8, LANES), F32),
            pltpu.VMEM((OWNERS, 8, LANES), F32),
            pltpu.VMEM((OWNERS, LANES), jnp.int32),
            pltpu.VMEM((LAYERS, CY, CX), F32),
            pltpu.SemaphoreType.DMA((3,)),
        ],
        name="main",
    )(*near(base, east, west, one, two, spots, moves), source_weights[0], source_counts[0])
    received = lax.all_to_all(
        partial_value, ("gx", "gy"), split_axis=0, concat_axis=0, tiled=True
    )
    obs_equiv = pl.pallas_call(
        owner_kernel,
        in_specs=[VMEM] * 2,
        out_specs=VMEM,
        out_shape=shape(OBS_DEV // LANES, LANES),
        name="owner",
    )(*near(received, slot_owner[0]))
    return smoothed.reshape(increments.shape), obs_equiv.reshape(-1)


def solution(mesh):
    return jax.shard_map(
        local,
        mesh=mesh,
        in_specs=(
            P(None, None, "gy", "gx"),
            P(None, "gy", "gx"),
            P("gy", "gx"),
            P(("gx", "gy"), None, None, None, None),
            P(("gx", "gy"), None, None, None),
            P(("gx", "gy"), None, None),
            P(("gx", "gy"), None, None),
        ),
        out_specs=(P(None, None, "gy", "gx"), P(("gx", "gy"))),
        check_vma=False,
    )
```

```python
import jax
import jax.numpy as jnp
from jax import lax
from jax.experimental import pallas as pl
from jax.experimental.pallas import tpu as pltpu
from jax.sharding import PartitionSpec as P

F32 = jnp.float32
BF16 = jnp.bfloat16
ITERS = 10
HALO = 10
OBS_DEV = 4096
LAYERS = 6
LEVELS = 3
ARRAYS = LAYERS + LEVELS
CY = 24
CX = 256
LANES = 128
STRIDE = 14
ROWS = 48
WIDE = 3
TABLE = LAYERS * CY * 2
MOST = 40
TURN = 16
LOOKED_UP = 5
BANDS = 6
UNROLL = 5
OWNERS = 128
STAGES = 10
STRIP = (HALO * (ARRAYS + 1), CX)
VMEM = pl.BlockSpec(memory_space=pltpu.VMEM)


def iota(shape, dim):
    return lax.broadcasted_iota(jnp.int32, shape, dim)


def pack_kernel(inc_ref, dif_ref, mask_ref, base_ref, first_ref, last_ref):
    wet = mask_ref[...].astype(F32)
    lane = iota((CY, LANES), 1)
    first = jnp.zeros((CY, LANES), F32)
    last = jnp.zeros((CY, LANES), F32)
    for a in range(ARRAYS):
        values = (inc_ref[a] if a < LAYERS else dif_ref[a - LAYERS]) * wet
        base_ref[a] = values
        mine = (lane >= STRIDE * a) & (lane < STRIDE * a + HALO)
        left = values[:, :LANES]
        right = values[:, LANES:]
        if a:
            left = pltpu.roll(left, STRIDE * a, 1)
        right = pltpu.roll(right, STRIDE * a + HALO, 1)
        first = jnp.where(mine, left, first)
        last = jnp.where(mine, right, last)
    first_ref[...] = first
    last_ref[...] = last


def rows_kernel(base_ref, east_ref, west_ref, one_ref, two_ref):
    even = lax.axis_index("gy") % 2 == 0

    def fill(ref, start):
        for a in range(ARRAYS):
            ref[pl.ds(HALO * a, HALO), :] = base_ref[a, pl.ds(start, HALO), :]
        ref[pl.ds(HALO * ARRAYS, HALO), pl.ds(0, LANES)] = east_ref[pl.ds(start, HALO), :]
        ref[pl.ds(HALO * ARRAYS, HALO), pl.ds(LANES, LANES)] = west_ref[pl.ds(start, HALO), :]

    @pl.when(even)
    def _():
        fill(one_ref, 0)
        fill(two_ref, CY - HALO)

    @pl.when(jnp.logical_not(even))
    def _():
        fill(one_ref, CY - HALO)
        fill(two_ref, 0)


def plan_kernel(cells_ref, counts_ref, spots_ref, moves_ref, first_ref, second_ref, shift_ref):
    before = (iota((OWNERS, OWNERS), 1) < iota((OWNERS, OWNERS), 0)).astype(F32).astype(BF16)
    held = counts_ref[...].astype(F32).astype(BF16)
    start = jnp.dot(before, held, preferred_element_type=F32).astype(jnp.int32)
    shift_ref[...] = 8 * iota((OWNERS, LANES), 0) - start
    sub_id = iota((8, LANES), 0)
    nothing = jnp.zeros((8, LANES), jnp.int32)
    for o in range(OWNERS):
        col = cells_ref[o, 2]
        row = (col >> 7) * (LAYERS * CY) + cells_ref[o, 0] * CY + cells_ref[o, 1]
        spot = (shift_ref[pl.ds(o, 8, stride=0), :] << 16) + (row << 7) + (col & (LANES - 1))
        first_ref[o] = jnp.where(sub_id < counts_ref[pl.ds(o, 8, stride=0), :], spot, 0)
        moves_ref[o] = nothing
    old_ref, new_ref = first_ref, second_ref
    for bit in range(STAGES):
        jump = 1 << bit
        mark = 1 << (16 + bit)
        if bit == STAGES - 1:
            new_ref = spots_ref
        turned = None
        for o in range(OWNERS):
            here = old_ref[o]
            if bit >= 3:
                source = o + (jump >> 3)
                there = old_ref[source] if source < OWNERS else nothing
            else:
                if turned is None:
                    turned = pltpu.roll(here, 8 - jump, 0)
                after = pltpu.roll(old_ref[o + 1], 8 - jump, 0) if o + 1 < OWNERS else nothing
                there = jnp.where(sub_id < 8 - jump, turned, after)
                turned = after
            goes = here & mark
            moves_ref[o] = moves_ref[o] | (goes >> 16)
            new_ref[o] = jnp.where((there & mark) != 0, there, jnp.where(goes != 0, 0, here))
        old_ref, new_ref = new_ref, old_ref


def smooth(
    base_ref, east_ref, west_ref, north_ref, south_ref, out_ref, wide_ref, coeff_ref,
    table_ref,
):
    lane_tile = iota((CY, LANES), 1)
    lane_rows = iota((HALO, LANES), 1)

    def side(east, west, a, lane):
        if a:
            east = pltpu.roll(east, LANES - STRIDE * a, 1)
        west = pltpu.roll(west, (LANES - HALO - STRIDE * a) % LANES, 1)
        halo = jnp.where(lane < HALO, east, 0.0)
        return jnp.where(lane >= LANES - HALO, west, halo)

    strip = pl.ds(HALO * ARRAYS, HALO)
    for a in range(ARRAYS):
        for v in range(2):
            lanes = pl.ds(v * LANES, LANES)
            wide_ref[a, v, pl.ds(0, CY), :] = base_ref[a, :, lanes]
            wide_ref[a, v, pl.ds(CY, CY), :] = jnp.zeros((CY, LANES), F32)
            wide_ref[a, v, pl.ds(CY, HALO), :] = north_ref[pl.ds(HALO * a, HALO), lanes]
            wide_ref[a, v, pl.ds(ROWS - HALO, HALO), :] = south_ref[pl.ds(HALO * a, HALO), lanes]
        wide_ref[a, 2, pl.ds(0, CY), :] = side(east_ref[...], west_ref[...], a, lane_tile)
        wide_ref[a, 2, pl.ds(CY, CY), :] = jnp.zeros((CY, LANES), F32)
        for ref, start in ((north_ref, CY), (south_ref, ROWS - HALO)):
            wide_ref[a, 2, pl.ds(start, HALO), :] = side(
                ref[strip, pl.ds(0, LANES)], ref[strip, pl.ds(LANES, LANES)], a, lane_rows
            )

    lane = iota((8, LANES), 1)

    def bands(a):
        return [
            [wide_ref[a, v, pl.ds(b, 8, stride=BANDS), :] for v in range(WIDE)]
            for b in range(BANDS)
        ]

    def to_east(parts):
        turned = [pltpu.roll(part, LANES - 1, 1) for part in parts]
        return [
            jnp.where(lane == LANES - 1, turned[(v + 1) % WIDE], turned[v]) for v in range(WIDE)
        ]

    def to_west(parts):
        turned = [pltpu.roll(part, 1, 1) for part in parts]
        return [jnp.where(lane == 0, turned[(v - 1) % WIDE], turned[v]) for v in range(WIDE)]

    def to_north(values):
        return values[1:] + [[pltpu.roll(part, 7, 0) for part in values[0]]]

    def to_south(values):
        return [[pltpu.roll(part, 1, 0) for part in values[-1]]] + values[:-1]

    def face(here, there):
        return [
            jnp.where((x > 0.0) & (y > 0.0), 0.5 * (x + y), 0.0) for x, y in zip(here, there)
        ]

    for level in range(LEVELS):
        here = bands(LAYERS + level)
        north = [face(x, y) for x, y in zip(here, to_north(here))]
        south = to_south(north)
        for b in range(BANDS):
            east = face(here[b], to_east(here[b]))
            west = to_west(east)
            for v in range(WIDE):
                sides = (east[v], west[v], north[b][v], south[b][v])
                keep = 1.0 - ((sides[0] + sides[1]) + (sides[2] + sides[3]))
                for i, side_value in enumerate((keep,) + sides):
                    coeff_ref[level, i, b, v] = side_value

    def step(field, level):
        north = to_north(field)
        south = to_south(field)
        updated = []
        for b in range(BANDS):
            around = (field[b], to_east(field[b]), to_west(field[b]), north[b], south[b])
            parts = []
            for v in range(WIDE):
                terms = [coeff_ref[level, i, b, v] * near[v] for i, near in enumerate(around)]
                parts.append(terms[0] + ((terms[1] + terms[2]) + (terms[3] + terms[4])))
            updated.append(parts)
        return updated

    for level in range(LEVELS):

        def turn(_, fields):
            for _ in range(UNROLL):
                fields = [step(field, level) for field in fields]
            return fields

        pair = lax.fori_loop(0, ITERS // UNROLL, turn, [bands(level), bands(level + LEVELS)])
        for layer, field in zip((level, level + LEVELS), pair):
            for v in range(2):
                first = (v * LAYERS + layer) * CY
                for b in range(BANDS):
                    table_ref[pl.ds(first + b, CY // BANDS, stride=BANDS), :] = field[b][v][
                        :CY // BANDS
                    ]
                out_ref[layer, :, pl.ds(v * LANES, LANES)] = table_ref[pl.ds(first, CY), :]


def choose(parts, bits):
    turn = 0
    while len(parts) > 1:
        pairs = [
            jnp.where(bits[turn], parts[2 * j + 1], parts[2 * j]) for j in range(len(parts) // 2)
        ]
        parts = pairs + parts[2 * len(pairs):]
        turn += 1
    return parts[0]


def main_kernel(
    base_ref, east_ref, west_ref, one_ref, two_ref, spots_ref, moves_ref, weights_far, counts_far,
    smooth_far, partial_ref, wide_ref, coeff_ref, table_ref, split_ref, north_ref, south_ref,
    first_ref, second_ref, weights_ref, counts_ref, smooth_ref, arrived,
):
    fetches = [
        pltpu.make_async_copy(far, ref, arrived.at[i])
        for i, (far, ref) in enumerate(((weights_far, weights_ref), (counts_far, counts_ref)))
    ]
    for fetch in fetches:
        fetch.start()
    place = lax.axis_index("gy")
    even = place % 2 == 0
    edge = (place == 0) | (place == lax.axis_size("gy") - 1)
    one = jnp.where(edge, 0.0, one_ref[...])
    two = two_ref[...]
    north_ref[...] = jnp.where(even, two, one)
    south_ref[...] = jnp.where(even, one, two)
    smooth(
        base_ref, east_ref, west_ref, north_ref, south_ref, smooth_ref, wide_ref, coeff_ref,
        table_ref,
    )
    leave = pltpu.make_async_copy(smooth_ref, smooth_far, arrived.at[2])
    leave.start()
    values = table_ref[...]
    coarse = values.astype(BF16)
    split_ref[:, pl.ds(0, LANES)] = coarse
    split_ref[:, pl.ds(LANES, LANES)] = (values - coarse.astype(F32)).astype(BF16)

    for fetch in fetches:
        fetch.wait()
    counts = counts_ref[...]
    rows_used = jnp.max(jnp.sum(counts.astype(F32), axis=0, keepdims=True)).astype(jnp.int32)
    split = split_ref[...]
    lane_id = iota((LANES, LANES), 0).astype(BF16)
    sub_id = iota((8, LANES), 0)

    def places(o):
        spot = spots_ref[o] & 0xFFFF
        return spot >> 7, spot & (LANES - 1)

    def by_matmul(o):
        rows_at, lane_at = places(o)
        lane_at = lane_at.astype(F32).astype(BF16)
        result = jnp.zeros((8, LANES), F32)
        for k in range(0, 8, 2):
            picks = []
            for j in (k, k + 1):
                lane_row = jnp.broadcast_to(lane_at[j:j + 1, :], (LANES, LANES))
                picks.append(jnp.where(lane_id == lane_row, BF16(1), BF16(0)))
            pick = jnp.concatenate(picks, axis=1)
            found = jnp.dot(
                split, jnp.concatenate([pick, pick], axis=0), preferred_element_type=F32
            )
            for j in (0, 1):
                block = found[:, j * LANES:(j + 1) * LANES]
                at = jnp.broadcast_to(rows_at[k + j:k + j + 1, :], (8, LANES))
                bits = [(at & (8 << b)) != 0 for b in range(6)]
                value = choose([block[8 * q:8 * q + 8] for q in range(TABLE // 8)], bits)
                value = jnp.take_along_axis(value, at & 7, axis=0)
                result = jnp.where(sub_id == k + j, value, result)
        first_ref[o] = result

    def by_lanes(o):
        rows_at, lane_at = places(o)
        bits = [(rows_at & (1 << b)) != 0 for b in range(3)]
        found = jnp.zeros((8, LANES), F32)
        for q in range(TABLE // 8):
            rows = [table_ref[pl.ds(8 * q + r, 8, stride=0), :] for r in range(8)]
            value = choose([jnp.take_along_axis(row, lane_at, axis=1) for row in rows], bits)
            found = jnp.where((rows_at >> 3) == q, value, found)
        first_ref[o] = found

    def lookup(first, size, singles):
        for j in range(size - singles):
            by_matmul(first + j)
        for j in range(size - singles, size):
            by_lanes(first + j)

    def most(i, _):
        lookup(i * MOST, MOST, 13)
        return 0

    def rest(i, _):
        lookup(2 * MOST + i * TURN, TURN, LOOKED_UP)
        return 0

    lax.fori_loop(0, jnp.minimum((rows_used + (8 * MOST - 1)) // (8 * MOST), 2), most, 0)
    left = jnp.maximum(rows_used - 16 * MOST, 0)
    lax.fori_loop(0, (left + (8 * TURN - 1)) // (8 * TURN), rest, 0)

    old_ref, new_ref = first_ref, second_ref
    for bit in reversed(range(STAGES)):
        jump = 1 << bit
        turned = None
        for o in range(OWNERS):
            here = old_ref[o]
            if bit >= 3:
                source = o - (jump >> 3)
                there = old_ref[source] if source >= 0 else here
            else:
                now = pltpu.roll(here, jump, 0)
                there = now if turned is None else jnp.where(sub_id < jump, turned, now)
                turned = now
            new = jnp.where((moves_ref[o] & jump) != 0, there, here)
            if bit:
                new_ref[o] = new
            else:
                valid = sub_id < counts_ref[pl.ds(o, 8, stride=0), :]
                weighted = jnp.where(valid, weights_ref[o] * new, 0.0)
                partial_ref[o] = jnp.sum(weighted, axis=0, keepdims=True)
        old_ref, new_ref = new_ref, old_ref
    leave.wait()


def owner_kernel(values_ref, slots_ref, out_ref):
    high_id = iota((32, LANES), 0).astype(BF16)
    low_id = iota((LANES, LANES), 0).astype(BF16)
    slots = slots_ref[...]
    highs = (slots >> 7).astype(F32).astype(BF16)
    lows = (slots & (LANES - 1)).astype(F32).astype(BF16)
    none = jnp.zeros((32, LANES), BF16)
    total = jnp.zeros((LANES, 64), F32)
    for g in range(0, OWNERS, 8):
        left = []
        right = []
        for j in range(g, g + 8):
            value = values_ref[j]
            coarse = value.astype(BF16)
            fine = (value - coarse.astype(F32)).astype(BF16)
            high = high_id == jnp.broadcast_to(highs[j:j + 1, :], (32, LANES))
            low = low_id == jnp.broadcast_to(lows[j:j + 1, :], (LANES, LANES))
            parts = [
                jnp.where(high, jnp.broadcast_to(part, (32, LANES)), none)
                for part in (coarse, fine)
            ]
            right.append(jnp.concatenate(parts, axis=0))
            left.append(jnp.where(low, BF16(1), BF16(0)))
        total = total + lax.dot_general(
            jnp.concatenate(left, axis=1),
            jnp.concatenate(right, axis=1),
            (((1,), (1,)), ((), ())),
            preferred_element_type=F32,
        )
    total = total.T
    out_ref[...] = total[:32] + total[32:]


def shape(*dims):
    return jax.ShapeDtypeStruct(dims, F32)


def shift(array, axis, step):
    size = lax.axis_size(axis)
    return lax.ppermute(array, axis, [(i, (i + step) % size) for i in range(size)])


def pairs(array, axis, odd):
    size = lax.axis_size(axis)
    swaps = [(i, (((i + odd) % size) ^ 1) - odd) for i in range(size)]
    return lax.ppermute(array, axis, [(i, j % size) for i, j in swaps])


def near(*arrays):
    return [pltpu.with_memory_space_constraint(array, pltpu.MemorySpace.VMEM) for array in arrays]


def local(
    increments, diffusivity, sea_mask, source_cells, source_weights, source_counts, slot_owner
):
    base, first, last = pl.pallas_call(
        pack_kernel,
        in_specs=[VMEM] * 3,
        out_specs=(VMEM,) * 3,
        out_shape=(pltpu.VMEM((ARRAYS, CY, CX), F32),) + (pltpu.VMEM((CY, LANES), F32),) * 2,
        name="pack",
    )(increments.reshape(LAYERS, CY, CX), diffusivity, sea_mask)
    east = shift(first, "gx", -1)
    west = shift(last, "gx", 1)
    one, two = pl.pallas_call(
        rows_kernel,
        in_specs=[VMEM] * 3,
        out_specs=(VMEM,) * 2,
        out_shape=(pltpu.VMEM(STRIP, F32),) * 2,
        name="rows",
    )(*near(base, east, west))
    one = pairs(one, "gy", 1)
    two = pairs(two, "gy", 0)
    whole = pltpu.VMEM((OWNERS, 8, LANES), jnp.int32)
    spots, moves = pl.pallas_call(
        plan_kernel,
        in_specs=[VMEM] * 2,
        out_specs=(VMEM,) * 2,
        out_shape=(whole, whole),
        scratch_shapes=[whole, whole, pltpu.VMEM((OWNERS, LANES), jnp.int32)],
        name="plan",
    )(source_cells[0], source_counts[0])
    smoothed, partial_value = pl.pallas_call(
        main_kernel,
        in_specs=[VMEM] * 7 + [pl.BlockSpec(memory_space=pl.ANY)] * 2,
        out_specs=(pl.BlockSpec(memory_space=pl.ANY), VMEM),
        out_shape=(shape(LAYERS, CY, CX), pltpu.VMEM((OWNERS, 1, LANES), F32)),
        scratch_shapes=[
            pltpu.VMEM((ARRAYS, WIDE, ROWS, LANES), F32),
            pltpu.VMEM((LEVELS, 5, BANDS, WIDE, 8, LANES), F32),
            pltpu.VMEM((TABLE, LANES), F32),
            pltpu.VMEM((TABLE, 2 * LANES), BF16),
            pltpu.VMEM(STRIP, F32),
            pltpu.VMEM(STRIP, F32),
            pltpu.VMEM((OWNERS, 8, LANES), F32),
            pltpu.VMEM((OWNERS, 8, LANES), F32),
            pltpu.VMEM((OWNERS, 8, LANES), F32),
            pltpu.VMEM((OWNERS, LANES), jnp.int32),
            pltpu.VMEM((LAYERS, CY, CX), F32),
            pltpu.SemaphoreType.DMA((3,)),
        ],
        name="main",
    )(*near(base, east, west, one, two, spots, moves), source_weights[0], source_counts[0])
    received = lax.all_to_all(
        partial_value, ("gx", "gy"), split_axis=0, concat_axis=0, tiled=True
    )
    obs_equiv = pl.pallas_call(
        owner_kernel,
        in_specs=[VMEM] * 2,
        out_specs=VMEM,
        out_shape=shape(OBS_DEV // LANES, LANES),
        name="owner",
    )(*near(received, slot_owner[0]))
    return smoothed.reshape(increments.shape), obs_equiv.reshape(-1)


def solution(mesh):
    return jax.shard_map(
        local,
        mesh=mesh,
        in_specs=(
            P(None, None, "gy", "gx"),
            P(None, "gy", "gx"),
            P("gy", "gx"),
            P(("gx", "gy"), None, None, None, None),
            P(("gx", "gy"), None, None, None),
            P(("gx", "gy"), None, None),
            P(("gx", "gy"), None, None),
        ),
        out_specs=(P(None, None, "gy", "gx"), P(("gx", "gy"))),
        check_vma=False,
    )
```

```python
import jax
import jax.numpy as jnp
from jax import lax
from jax.experimental import pallas as pl
from jax.experimental.pallas import tpu as pltpu
from jax.sharding import PartitionSpec as P

F32 = jnp.float32
BF16 = jnp.bfloat16
ITERS = 10
HALO = 10
OBS_DEV = 4096
LAYERS = 6
LEVELS = 3
ARRAYS = LAYERS + LEVELS
CY = 24
CX = 256
LANES = 128
STRIDE = 14
ROWS = 48
WIDE = 3
TABLE = LAYERS * CY * 2
MOST = 40
TURN = 16
LOOKED_UP = 5
BANDS = 6
UNROLL = 5
OWNERS = 128
STAGES = 10
STRIP = (HALO * (ARRAYS + 1), CX)
VMEM = pl.BlockSpec(memory_space=pltpu.VMEM)


def iota(shape, dim):
    return lax.broadcasted_iota(jnp.int32, shape, dim)


def pack_kernel(inc_ref, dif_ref, mask_ref, base_ref, far_ref, close_ref):
    wet = mask_ref[...].astype(F32)
    lane = iota((CY, LANES), 1)
    first = jnp.zeros((CY, LANES), F32)
    last = jnp.zeros((CY, LANES), F32)
    for a in range(ARRAYS):
        values = (inc_ref[a] if a < LAYERS else dif_ref[a - LAYERS]) * wet
        base_ref[a] = values
        mine = (lane >= STRIDE * a) & (lane < STRIDE * a + HALO)
        left = values[:, :LANES]
        right = values[:, LANES:]
        if a:
            left = pltpu.roll(left, STRIDE * a, 1)
        right = pltpu.roll(right, STRIDE * a + HALO, 1)
        first = jnp.where(mine, left, first)
        last = jnp.where(mine, right, last)
    even = lax.axis_index("gx") % 2 == 0
    far_ref[...] = jnp.where(even, first, last)
    close_ref[...] = jnp.where(even, last, first)


def rows_kernel(base_ref, far_ref, close_ref, one_ref, two_ref, east_ref, west_ref):
    even_x = lax.axis_index("gx") % 2 == 0
    east_ref[...] = jnp.where(even_x, close_ref[...], far_ref[...])
    west_ref[...] = jnp.where(even_x, far_ref[...], close_ref[...])
    even = lax.axis_index("gy") % 2 == 0

    def fill(ref, start):
        for a in range(ARRAYS):
            ref[pl.ds(HALO * a, HALO), :] = base_ref[a, pl.ds(start, HALO), :]
        ref[pl.ds(HALO * ARRAYS, HALO), pl.ds(0, LANES)] = east_ref[pl.ds(start, HALO), :]
        ref[pl.ds(HALO * ARRAYS, HALO), pl.ds(LANES, LANES)] = west_ref[pl.ds(start, HALO), :]

    @pl.when(even)
    def _():
        fill(one_ref, 0)
        fill(two_ref, CY - HALO)

    @pl.when(jnp.logical_not(even))
    def _():
        fill(one_ref, CY - HALO)
        fill(two_ref, 0)


def plan_kernel(cells_ref, counts_ref, spots_ref, moves_ref, first_ref, second_ref, shift_ref):
    before = (iota((OWNERS, OWNERS), 1) < iota((OWNERS, OWNERS), 0)).astype(F32).astype(BF16)
    held = counts_ref[...].astype(F32).astype(BF16)
    start = jnp.dot(before, held, preferred_element_type=F32).astype(jnp.int32)
    shift_ref[...] = 8 * iota((OWNERS, LANES), 0) - start
    sub_id = iota((8, LANES), 0)
    nothing = jnp.zeros((8, LANES), jnp.int32)
    for o in range(OWNERS):
        col = cells_ref[o, 2]
        row = (col >> 7) * (LAYERS * CY) + cells_ref[o, 0] * CY + cells_ref[o, 1]
        spot = (shift_ref[pl.ds(o, 8, stride=0), :] << 16) + (row << 7) + (col & (LANES - 1))
        first_ref[o] = jnp.where(sub_id < counts_ref[pl.ds(o, 8, stride=0), :], spot, 0)
        moves_ref[o] = nothing
    old_ref, new_ref = first_ref, second_ref
    for bit in range(STAGES):
        jump = 1 << bit
        mark = 1 << (16 + bit)
        if bit == STAGES - 1:
            new_ref = spots_ref
        turned = None
        for o in range(OWNERS):
            here = old_ref[o]
            if bit >= 3:
                source = o + (jump >> 3)
                there = old_ref[source] if source < OWNERS else nothing
            else:
                if turned is None:
                    turned = pltpu.roll(here, 8 - jump, 0)
                after = pltpu.roll(old_ref[o + 1], 8 - jump, 0) if o + 1 < OWNERS else nothing
                there = jnp.where(sub_id < 8 - jump, turned, after)
                turned = after
            goes = here & mark
            moves_ref[o] = moves_ref[o] | (goes >> 16)
            new_ref[o] = jnp.where((there & mark) != 0, there, jnp.where(goes != 0, 0, here))
        old_ref, new_ref = new_ref, old_ref


def smooth(
    base_ref, east_ref, west_ref, north_ref, south_ref, out_ref, wide_ref, coeff_ref,
    table_ref,
):
    lane_tile = iota((CY, LANES), 1)
    lane_rows = iota((HALO, LANES), 1)

    def side(east, west, a, lane):
        if a:
            east = pltpu.roll(east, LANES - STRIDE * a, 1)
        west = pltpu.roll(west, (LANES - HALO - STRIDE * a) % LANES, 1)
        halo = jnp.where(lane < HALO, east, 0.0)
        return jnp.where(lane >= LANES - HALO, west, halo)

    strip = pl.ds(HALO * ARRAYS, HALO)
    for a in range(ARRAYS):
        for v in range(2):
            lanes = pl.ds(v * LANES, LANES)
            wide_ref[a, v, pl.ds(0, CY), :] = base_ref[a, :, lanes]
            wide_ref[a, v, pl.ds(CY, CY), :] = jnp.zeros((CY, LANES), F32)
            wide_ref[a, v, pl.ds(CY, HALO), :] = north_ref[pl.ds(HALO * a, HALO), lanes]
            wide_ref[a, v, pl.ds(ROWS - HALO, HALO), :] = south_ref[pl.ds(HALO * a, HALO), lanes]
        wide_ref[a, 2, pl.ds(0, CY), :] = side(east_ref[...], west_ref[...], a, lane_tile)
        wide_ref[a, 2, pl.ds(CY, CY), :] = jnp.zeros((CY, LANES), F32)
        for ref, start in ((north_ref, CY), (south_ref, ROWS - HALO)):
            wide_ref[a, 2, pl.ds(start, HALO), :] = side(
                ref[strip, pl.ds(0, LANES)], ref[strip, pl.ds(LANES, LANES)], a, lane_rows
            )

    lane = iota((8, LANES), 1)

    def bands(a):
        return [
            [wide_ref[a, v, pl.ds(b, 8, stride=BANDS), :] for v in range(WIDE)]
            for b in range(BANDS)
        ]

    def to_east(parts):
        turned = [pltpu.roll(part, LANES - 1, 1) for part in parts]
        return [
            jnp.where(lane == LANES - 1, turned[(v + 1) % WIDE], turned[v]) for v in range(WIDE)
        ]

    def to_west(parts):
        turned = [pltpu.roll(part, 1, 1) for part in parts]
        return [jnp.where(lane == 0, turned[(v - 1) % WIDE], turned[v]) for v in range(WIDE)]

    def to_north(values):
        return values[1:] + [[pltpu.roll(part, 7, 0) for part in values[0]]]

    def to_south(values):
        return [[pltpu.roll(part, 1, 0) for part in values[-1]]] + values[:-1]

    def face(here, there):
        return [
            jnp.where((x > 0.0) & (y > 0.0), 0.5 * (x + y), 0.0) for x, y in zip(here, there)
        ]

    for level in range(LEVELS):
        here = bands(LAYERS + level)
        north = [face(x, y) for x, y in zip(here, to_north(here))]
        south = to_south(north)
        for b in range(BANDS):
            east = face(here[b], to_east(here[b]))
            west = to_west(east)
            for v in range(WIDE):
                sides = (east[v], west[v], north[b][v], south[b][v])
                keep = 1.0 - ((sides[0] + sides[1]) + (sides[2] + sides[3]))
                for i, side_value in enumerate((keep,) + sides):
                    coeff_ref[level, i, b, v] = side_value

    def step(field, level):
        north = to_north(field)
        south = to_south(field)
        updated = []
        for b in range(BANDS):
            around = (field[b], to_east(field[b]), to_west(field[b]), north[b], south[b])
            parts = []
            for v in range(WIDE):
                terms = [coeff_ref[level, i, b, v] * near[v] for i, near in enumerate(around)]
                parts.append(terms[0] + ((terms[1] + terms[2]) + (terms[3] + terms[4])))
            updated.append(parts)
        return updated

    for level in range(LEVELS):

        def turn(_, fields):
            for _ in range(UNROLL):
                fields = [step(field, level) for field in fields]
            return fields

        pair = lax.fori_loop(0, ITERS // UNROLL, turn, [bands(level), bands(level + LEVELS)])
        for layer, field in zip((level, level + LEVELS), pair):
            for v in range(2):
                first = (v * LAYERS + layer) * CY
                for b in range(BANDS):
                    table_ref[pl.ds(first + b, CY // BANDS, stride=BANDS), :] = field[b][v][
                        :CY // BANDS
                    ]
                out_ref[layer, :, pl.ds(v * LANES, LANES)] = table_ref[pl.ds(first, CY), :]


def choose(parts, bits):
    turn = 0
    while len(parts) > 1:
        pairs = [
            jnp.where(bits[turn], parts[2 * j + 1], parts[2 * j]) for j in range(len(parts) // 2)
        ]
        parts = pairs + parts[2 * len(pairs):]
        turn += 1
    return parts[0]


def main_kernel(
    base_ref, east_ref, west_ref, one_ref, two_ref, spots_ref, moves_ref, weights_far, counts_far,
    smooth_far, partial_ref, wide_ref, coeff_ref, table_ref, split_ref, north_ref, south_ref,
    first_ref, second_ref, weights_ref, counts_ref, smooth_ref, arrived,
):
    fetches = [
        pltpu.make_async_copy(far, ref, arrived.at[i])
        for i, (far, ref) in enumerate(((weights_far, weights_ref), (counts_far, counts_ref)))
    ]
    for fetch in fetches:
        fetch.start()
    place = lax.axis_index("gy")
    even = place % 2 == 0
    edge = (place == 0) | (place == lax.axis_size("gy") - 1)
    one = jnp.where(edge, 0.0, one_ref[...])
    two = two_ref[...]
    north_ref[...] = jnp.where(even, two, one)
    south_ref[...] = jnp.where(even, one, two)
    smooth(
        base_ref, east_ref, west_ref, north_ref, south_ref, smooth_ref, wide_ref, coeff_ref,
        table_ref,
    )
    leave = pltpu.make_async_copy(smooth_ref, smooth_far, arrived.at[2])
    leave.start()
    values = table_ref[...]
    coarse = values.astype(BF16)
    split_ref[:, pl.ds(0, LANES)] = coarse
    split_ref[:, pl.ds(LANES, LANES)] = (values - coarse.astype(F32)).astype(BF16)

    for fetch in fetches:
        fetch.wait()
    counts = counts_ref[...]
    rows_used = jnp.max(jnp.sum(counts.astype(F32), axis=0, keepdims=True)).astype(jnp.int32)
    split = split_ref[...]
    lane_id = iota((LANES, LANES), 0).astype(BF16)
    sub_id = iota((8, LANES), 0)

    def places(o):
        spot = spots_ref[o] & 0xFFFF
        return spot >> 7, spot & (LANES - 1)

    def by_matmul(o):
        rows_at, lane_at = places(o)
        lane_at = lane_at.astype(F32).astype(BF16)
        result = jnp.zeros((8, LANES), F32)
        for k in range(0, 8, 2):
            picks = []
            for j in (k, k + 1):
                lane_row = jnp.broadcast_to(lane_at[j:j + 1, :], (LANES, LANES))
                picks.append(jnp.where(lane_id == lane_row, BF16(1), BF16(0)))
            pick = jnp.concatenate(picks, axis=1)
            found = jnp.dot(
                split, jnp.concatenate([pick, pick], axis=0), preferred_element_type=F32
            )
            for j in (0, 1):
                block = found[:, j * LANES:(j + 1) * LANES]
                at = jnp.broadcast_to(rows_at[k + j:k + j + 1, :], (8, LANES))
                bits = [(at & (8 << b)) != 0 for b in range(6)]
                value = choose([block[8 * q:8 * q + 8] for q in range(TABLE // 8)], bits)
                value = jnp.take_along_axis(value, at & 7, axis=0)
                result = jnp.where(sub_id == k + j, value, result)
        first_ref[o] = result

    def by_lanes(o):
        rows_at, lane_at = places(o)
        bits = [(rows_at & (1 << b)) != 0 for b in range(3)]
        found = jnp.zeros((8, LANES), F32)
        for q in range(TABLE // 8):
            rows = [table_ref[pl.ds(8 * q + r, 8, stride=0), :] for r in range(8)]
            value = choose([jnp.take_along_axis(row, lane_at, axis=1) for row in rows], bits)
            found = jnp.where((rows_at >> 3) == q, value, found)
        first_ref[o] = found

    def lookup(first, size, singles):
        for j in range(size - singles):
            by_matmul(first + j)
        for j in range(size - singles, size):
            by_lanes(first + j)

    def most(i, _):
        lookup(i * MOST, MOST, 13)
        return 0

    def rest(i, _):
        lookup(2 * MOST + i * TURN, TURN, LOOKED_UP)
        return 0

    lax.fori_loop(0, jnp.minimum((rows_used + (8 * MOST - 1)) // (8 * MOST), 2), most, 0)
    left = jnp.maximum(rows_used - 16 * MOST, 0)
    lax.fori_loop(0, (left + (8 * TURN - 1)) // (8 * TURN), rest, 0)

    old_ref, new_ref = first_ref, second_ref
    for bit in reversed(range(STAGES)):
        jump = 1 << bit
        turned = None
        for o in range(OWNERS):
            here = old_ref[o]
            if bit >= 3:
                source = o - (jump >> 3)
                there = old_ref[source] if source >= 0 else here
            else:
                now = pltpu.roll(here, jump, 0)
                there = now if turned is None else jnp.where(sub_id < jump, turned, now)
                turned = now
            new = jnp.where((moves_ref[o] & jump) != 0, there, here)
            if bit:
                new_ref[o] = new
            else:
                valid = sub_id < counts_ref[pl.ds(o, 8, stride=0), :]
                weighted = jnp.where(valid, weights_ref[o] * new, 0.0)
                partial_ref[o] = jnp.sum(weighted, axis=0, keepdims=True)
        old_ref, new_ref = new_ref, old_ref
    leave.wait()


def owner_kernel(values_ref, slots_ref, out_ref):
    high_id = iota((32, LANES), 0).astype(BF16)
    low_id = iota((LANES, LANES), 0).astype(BF16)
    slots = slots_ref[...]
    highs = (slots >> 7).astype(F32).astype(BF16)
    lows = (slots & (LANES - 1)).astype(F32).astype(BF16)
    none = jnp.zeros((32, LANES), BF16)
    total = jnp.zeros((LANES, 64), F32)
    for g in range(0, OWNERS, 8):
        left = []
        right = []
        for j in range(g, g + 8):
            value = values_ref[j]
            coarse = value.astype(BF16)
            fine = (value - coarse.astype(F32)).astype(BF16)
            high = high_id == jnp.broadcast_to(highs[j:j + 1, :], (32, LANES))
            low = low_id == jnp.broadcast_to(lows[j:j + 1, :], (LANES, LANES))
            parts = [
                jnp.where(high, jnp.broadcast_to(part, (32, LANES)), none)
                for part in (coarse, fine)
            ]
            right.append(jnp.concatenate(parts, axis=0))
            left.append(jnp.where(low, BF16(1), BF16(0)))
        total = total + lax.dot_general(
            jnp.concatenate(left, axis=1),
            jnp.concatenate(right, axis=1),
            (((1,), (1,)), ((), ())),
            preferred_element_type=F32,
        )
    total = total.T
    out_ref[...] = total[:32] + total[32:]


def shape(*dims):
    return jax.ShapeDtypeStruct(dims, F32)


def pairs(array, axis, odd):
    size = lax.axis_size(axis)
    swaps = [(i, (((i + odd) % size) ^ 1) - odd) for i in range(size)]
    return lax.ppermute(array, axis, [(i, j % size) for i, j in swaps])


def near(*arrays):
    return [pltpu.with_memory_space_constraint(array, pltpu.MemorySpace.VMEM) for array in arrays]


def local(
    increments, diffusivity, sea_mask, source_cells, source_weights, source_counts, slot_owner
):
    base, far, close = pl.pallas_call(
        pack_kernel,
        in_specs=[VMEM] * 3,
        out_specs=(VMEM,) * 3,
        out_shape=(pltpu.VMEM((ARRAYS, CY, CX), F32),) + (pltpu.VMEM((CY, LANES), F32),) * 2,
        name="pack",
    )(increments.reshape(LAYERS, CY, CX), diffusivity, sea_mask)
    far = pairs(far, "gx", 1)
    close = pairs(close, "gx", 0)
    one, two, east, west = pl.pallas_call(
        rows_kernel,
        in_specs=[VMEM] * 3,
        out_specs=(VMEM,) * 4,
        out_shape=(pltpu.VMEM(STRIP, F32),) * 2 + (pltpu.VMEM((CY, LANES), F32),) * 2,
        name="rows",
    )(*near(base, far, close))
    one = pairs(one, "gy", 1)
    two = pairs(two, "gy", 0)
    whole = pltpu.VMEM((OWNERS, 8, LANES), jnp.int32)
    spots, moves = pl.pallas_call(
        plan_kernel,
        in_specs=[VMEM] * 2,
        out_specs=(VMEM,) * 2,
        out_shape=(whole, whole),
        scratch_shapes=[whole, whole, pltpu.VMEM((OWNERS, LANES), jnp.int32)],
        name="plan",
    )(source_cells[0], source_counts[0])
    smoothed, partial_value = pl.pallas_call(
        main_kernel,
        in_specs=[VMEM] * 7 + [pl.BlockSpec(memory_space=pl.ANY)] * 2,
        out_specs=(pl.BlockSpec(memory_space=pl.ANY), VMEM),
        out_shape=(shape(LAYERS, CY, CX), pltpu.VMEM((OWNERS, 1, LANES), F32)),
        scratch_shapes=[
            pltpu.VMEM((ARRAYS, WIDE, ROWS, LANES), F32),
            pltpu.VMEM((LEVELS, 5, BANDS, WIDE, 8, LANES), F32),
            pltpu.VMEM((TABLE, LANES), F32),
            pltpu.VMEM((TABLE, 2 * LANES), BF16),
            pltpu.VMEM(STRIP, F32),
            pltpu.VMEM(STRIP, F32),
            pltpu.VMEM((OWNERS, 8, LANES), F32),
            pltpu.VMEM((OWNERS, 8, LANES), F32),
            pltpu.VMEM((OWNERS, 8, LANES), F32),
            pltpu.VMEM((OWNERS, LANES), jnp.int32),
            pltpu.VMEM((LAYERS, CY, CX), F32),
            pltpu.SemaphoreType.DMA((3,)),
        ],
        name="main",
    )(*near(base, east, west, one, two, spots, moves), source_weights[0], source_counts[0])
    received = lax.all_to_all(
        partial_value, ("gx", "gy"), split_axis=0, concat_axis=0, tiled=True
    )
    obs_equiv = pl.pallas_call(
        owner_kernel,
        in_specs=[VMEM] * 2,
        out_specs=VMEM,
        out_shape=shape(OBS_DEV // LANES, LANES),
        name="owner",
    )(*near(received, slot_owner[0]))
    return smoothed.reshape(increments.shape), obs_equiv.reshape(-1)


def solution(mesh):
    return jax.shard_map(
        local,
        mesh=mesh,
        in_specs=(
            P(None, None, "gy", "gx"),
            P(None, "gy", "gx"),
            P("gy", "gx"),
            P(("gx", "gy"), None, None, None, None),
            P(("gx", "gy"), None, None, None),
            P(("gx", "gy"), None, None),
            P(("gx", "gy"), None, None),
        ),
        out_specs=(P(None, None, "gy", "gx"), P(("gx", "gy"))),
        check_vma=False,
    )
```
